32 devices in a mesh: dom: 16 (over z, y, x), orb: 2 (over core).
Axes of the slice: x: 2, y: 2, z: 4, core: 2. Of those that a mesh axis runs over, the one named last changes fastest.
Arguments:
- orbitals: bfloat16 [768, 64, 512], P('dom', 'orb'), may hold values from -6 to 6
- adjoint_source: bfloat16 [768, 64, 512], P('dom', 'orb'), may hold values from -6 to 6
- eigenvalues: float32 [64], P('orb'), may hold values from -1 to -0.25
- cell_scale: float32 [768], P('dom'), may hold values from 0.4 to 1.6
- base_potential: float32 [768, 512], P('dom'), may hold values from 0.5 to 1.5
- stiffness: bfloat16 [512, 512], replicated, may hold values from -1.5 to 1.5, as said below
- face_perm: int32 [768, 64], P('dom'), may hold values from 0 to 63, each once within a row
- restrict: bfloat16 [512, 64], replicated, may hold values from -0.25 to 0.25
- prolong: bfloat16 [64, 512], replicated, may hold values from -0.75 to 0.75
- owner: int32 [768, 1], P('dom'), may hold values from 0 to 15; in each aligned block of 48 rows (0 to 47, 48 to 95, ...) at most 6 rows name the same one
- pot_slot: int32 [768], P('dom'), may hold values from 0 to 63
- potential: float32 [1024, 64], P('dom'), may hold values from -6 to 6
Outputs:
- adjoint: bfloat16 [768, 64, 512], P('dom', 'orb')
- updated: float32 [1024, 64], P('dom')
- applied: bfloat16 [768, 64, 512], P('dom', 'orb')
The draws below stay inside these ranges and needn't reach their ends.
Inputs may be any that keep to these rules, and one draw needn't show every extreme that they name: In the rows of one device no owner is named by more than 6 cells. `face_perm`: each row is a permutation. `stiffness`: symmetric.
All inputs are finite; a program needn't handle non-finite values.
Results may differ from the reference program's by a relative error of at most 0.0027.
Values sent between devices are 32-bit elements; how exact they have to be, the bound alone decides.
A program may use at most 64 MiB of HBM per device.

```python
import math
import jax
import jax.numpy as jnp
import numpy as np
from jax import lax

P_SIZE = 512
FACE = 64
PN = 64
ORB = 64
CELL_DEV = 48
CELLS = 768
POT_DEV = 64
POT_CELLS = 1024
CAP = 6
ITERS = 4
N_DOM = 16


def draw_stiffness(key, part):
    key_diag, key_noise = jax.random.split(jax.random.fold_in(key, 11))
    diagonal = jax.random.uniform(key_diag, (P_SIZE,), jnp.float32, 0.8, 1.2)
    noise = jax.random.normal(key_noise, (P_SIZE, P_SIZE), jnp.float32) * (0.25 / P_SIZE ** 0.5)
    symmetric = (noise + noise.T) * 0.5 ** 0.5
    return (symmetric + jnp.diag(diagonal)).astype(jnp.bfloat16)


def plant(values, own_key, least, top_value):
    dims = values.shape
    spot = [jax.random.randint(jax.random.fold_in(own_key, axis), (), 0, dims[axis]) for axis in range(len(dims))]
    values = values.at[tuple(spot)].set(least)
    longest = dims.index(max(dims))
    spot[longest] = (spot[longest] + 1) % dims[longest]
    return values.at[tuple(spot)].set(top_value)


def block_levels(own_key, shape, cuts, smallest, top_value):
    def one(axis_at, blocks):
        heights = jax.random.uniform(jax.random.fold_in(jax.random.fold_in(own_key, 6), axis_at), (blocks,), jnp.float32, smallest / len(cuts), top_value / len(cuts))
        return jnp.repeat(jnp.exp(heights), shape[axis_at] // blocks).reshape((-1,) + (1,) * (len(shape) - axis_at - 1))

    factor_of = one(*cuts[0])
    for cut in cuts[1:]:
        factor_of = factor_of * one(*cut)
    return factor_of


def assign_block(own_key, own, number, rows, number_of, top, bound, skew):
    ranking = jax.random.permutation(own_key, number_of)
    packed, common = load_shares(number_of, rows * top, bound, skew, True), load_shares(number_of, rows * top, bound, skew, False)
    places = jnp.arange(number_of)

    def named(tallies, offset_by):
        used = int((tallies > 0).sum())
        fixed = max(1, used // 4)
        passed = fixed + (places - fixed + offset_by * (used - fixed)) % max(1, number_of - fixed)
        return jnp.zeros((number_of,), jnp.int32).at[ranking[jnp.where(places < fixed, places, passed)]].set(jnp.asarray(tallies, jnp.int32))

    tallies = jnp.where(number % 4 == 0, named(packed, number // 4), named(common, number - number // 4 - 1))
    mixed = jax.random.permutation(jax.random.fold_in(own, 3), number_of)
    source_of, receiver = mixed[0:number_of // 2 * 2:2], mixed[1:number_of // 2 * 2:2]
    room = jnp.minimum(tallies[source_of] - 1, bound - tallies[receiver]) // 2
    room = jnp.where((source_of == ranking[0]) | (receiver == ranking[0]) | (tallies[receiver] == 0), 0, jnp.maximum(room, 0))
    passed = jax.random.randint(jax.random.fold_in(own, 4), (number_of // 2,), 0, 1 << 20) % (room + 1)
    tallies = tallies.at[source_of].add(-passed).at[receiver].add(passed)
    members = jnp.searchsorted(jnp.cumsum(tallies), jnp.arange(rows * top), side="right").astype(jnp.int32)
    table = members.reshape(top, rows).T
    table = table[jax.random.permutation(jax.random.fold_in(own, 1), rows)]
    offset_by = jax.random.randint(jax.random.fold_in(own, 2), (rows, 1), 0, top)
    return jnp.take_along_axis(table, (jnp.arange(top)[None, :] + offset_by) % top, axis=1)


def load_shares(number_of, total, bound, slope, full):
    loads = [(1 << 20) // math.isqrt(rank ** slope) + 1 for rank in range(1, number_of + 1)]
    largest = bound if full else min(bound, max(-(-total // number_of), total * loads[0] // sum(loads)))
    least = 1 if total - largest >= number_of - 1 else 0
    holding, spare = [largest] + [least] * (number_of - 1), total - largest - least * (number_of - 1)
    while spare > 0:
        free = [i for i in range(1, number_of) if holding[i] < largest] or [i for i in range(1, number_of) if holding[i] < bound]
        pool, budget = sum([loads[i] for i in free]), spare
        for i in free:
            addition = min(bound - holding[i], max(1, budget * loads[i] // pool), spare)
            holding[i] = holding[i] + addition
            spare = spare - addition
    return np.array(holding)


def normal_values(key, extent, spread, reach, shards=(), kind=jnp.bfloat16):
    loudness = block_levels(key, extent, shards, -0.22, 0.18) if shards else 1.0
    values = jax.random.normal(key, extent, jnp.float32) * spread * loudness
    return jnp.minimum(jnp.maximum(values, -reach), reach).astype(kind)


def setup_inputs(seed: int = 0) -> dict:
    keys = jax.random.split(jax.random.key(seed), 13)
    orbitals = normal_values(keys[0], (CELLS, ORB, P_SIZE), 1.0, 6.0, ((0, 16), (1, 2)))
    adjoint_source = normal_values(keys[1], (CELLS, ORB, P_SIZE), 1.0, 6.0, ((0, 16), (1, 2)))
    eigenvalues = jnp.clip(-1.0 + 0.75 * jax.random.uniform(keys[2], (ORB,), jnp.float32) ** block_levels(keys[2], (ORB,), ((0, 2),), -0.2, 0.2), -1.0, -0.25)
    cell_scale = jnp.clip(jnp.exp(math.log(1.6) - 1.3862944 * jax.random.uniform(keys[3], (CELLS,), jnp.float32) ** block_levels(keys[3], (CELLS,), ((0, 16),), -0.2, 0.2)), 0.4, 1.6)
    base_potential = jnp.clip(0.5 + 1.0 * jax.random.uniform(keys[4], (CELLS, P_SIZE), jnp.float32) ** block_levels(keys[4], (CELLS, P_SIZE), ((0, 16),), -0.2, 0.2), 0.5, 1.5)
    stiffness = draw_stiffness(jax.random.fold_in(keys[12], 71), 0)
    face_perm = jax.vmap(lambda own: jax.random.permutation(own, FACE))(jax.random.split(keys[6], CELLS)).reshape((CELLS, FACE)).astype(jnp.int32)
    restrict = normal_values(keys[7], (P_SIZE, PN), P_SIZE ** -0.5, 0.25)
    prolong = normal_values(keys[8], (PN, P_SIZE), PN ** -0.5, 0.75)
    owner_keys = jax.random.split(jax.random.fold_in(keys[9], 1), CELLS // CELL_DEV)
    owner_turns = jax.random.permutation(jax.random.fold_in(keys[9], 3), CELLS // CELL_DEV)
    owner = jax.vmap(lambda own, number: assign_block(jax.random.fold_in(keys[9], 2), own, number, CELL_DEV, N_DOM, 1, CAP, 2))(owner_keys, owner_turns).reshape((CELLS, 1))
    pot_slot = plant(jax.random.randint(keys[10], (CELLS,), 0, POT_DEV), jax.random.fold_in(keys[10], 1), 0, POT_DEV - 1).astype(jnp.int32)
    potential = normal_values(keys[11], (POT_CELLS, PN), 1.0, 6.0, ((0, 16),), jnp.float32)
    return dict(orbitals=orbitals, adjoint_source=adjoint_source, eigenvalues=eigenvalues, cell_scale=cell_scale, base_potential=base_potential, stiffness=stiffness, face_perm=face_perm, restrict=restrict, prolong=prolong, owner=owner, pot_slot=pot_slot, potential=potential)


relax = 0.25
step_rate = 0.1


def face_onehot(face_perm):
    faces = face_perm.shape[1]
    return (face_perm[:, :, None] == jnp.arange(faces, dtype=jnp.int32)[None, None, :]).astype(jnp.float32)


def assemble(partial_sum, onehot):
    faces = onehot.shape[1]
    nodes = partial_sum.shape[2]
    left_face = partial_sum[:, :, :faces]
    right_face = partial_sum[:, :, nodes - faces:]
    sent_right = jnp.einsum('ckj,cok->coj', onehot, right_face, precision=lax.Precision.HIGHEST)
    zero_face = jnp.zeros_like(left_face[:1])
    left_next = jnp.concatenate([left_face[1:], zero_face], 0)
    add_right = jnp.einsum('ckj,coj->cok', onehot, left_next, precision=lax.Precision.HIGHEST)
    add_left = jnp.concatenate([zero_face, sent_right[:-1]], 0)
    return jnp.concatenate([left_face + add_left, partial_sum[:, :, faces:nodes - faces], right_face + add_right], 2)


def cell_operator(values_bf, values_full, shift, cell_scale, stiffness, onehot):
    nodes = stiffness.shape[0]
    kinetic = jnp.dot(values_bf.reshape(-1, nodes), stiffness, preferred_element_type=jnp.float32).reshape(values_full.shape)
    partial_sum = cell_scale[:, None, None] * kinetic + shift * values_full
    return assemble(partial_sum, onehot)


def reference(orbitals, adjoint_source, eigenvalues, cell_scale, base_potential, stiffness, face_perm, restrict, prolong, owner, pot_slot, potential):
    onehot = face_onehot(face_perm)
    width = min(8, ORB)
    blocks = ORB // width

    def solve_block(index):
        start = (index * width).astype(jnp.int32)
        psi_block = lax.dynamic_slice_in_dim(orbitals, start, width, 1)
        source_block = lax.dynamic_slice_in_dim(adjoint_source, start, width, 1).astype(jnp.float32)
        eig_block = lax.dynamic_slice_in_dim(eigenvalues, start, width, 0)
        shift = base_potential[:, None, :] - eig_block[None, :, None]
        iterate = relax * source_block
        for step_index in range(ITERS):
            image = cell_operator(iterate.astype(jnp.bfloat16), iterate, shift, cell_scale, stiffness, onehot)
            iterate = iterate + relax * (source_block - image)
        product = jnp.sum(psi_block.astype(jnp.float32) * iterate, axis=1)
        return iterate.astype(jnp.bfloat16), product

    adjoint_blocks, products = lax.map(solve_block, jnp.arange(blocks, dtype=jnp.int32))
    adjoint = jnp.transpose(adjoint_blocks, (1, 0, 2, 3)).reshape(CELLS, ORB, P_SIZE)
    density_term = jnp.sum(products, 0)
    projected = jnp.dot(density_term, restrict.astype(jnp.float32), precision=lax.Precision.HIGHEST)
    target = (owner[:, 0] * POT_DEV + pot_slot).astype(jnp.int32)
    summed = jax.ops.segment_sum(projected, target, num_segments=POT_DEV * N_DOM)
    updated = potential - step_rate * summed
    cell_pot = updated[target]
    node_potential = jnp.dot(cell_pot, prolong.astype(jnp.float32), precision=lax.Precision.HIGHEST)
    shift_new = (base_potential + node_potential)[:, None, :]

    def apply_block(index):
        start = (index * width).astype(jnp.int32)
        psi_block = lax.dynamic_slice_in_dim(orbitals, start, width, 1)
        result = cell_operator(psi_block, psi_block.astype(jnp.float32), shift_new, cell_scale, stiffness, onehot)
        return result.astype(jnp.bfloat16)

    applied_blocks = lax.map(apply_block, jnp.arange(blocks, dtype=jnp.int32))
    applied = jnp.transpose(applied_blocks, (1, 0, 2, 3)).reshape(CELLS, ORB, P_SIZE)
    return adjoint, updated, applied
```

```python
import functools

import jax
import jax.numpy as jnp
from jax import lax
from jax.experimental import pallas as pl
from jax.experimental.pallas import tpu as pltpu
from jax.sharding import PartitionSpec as P

ITERS = 4


relax = 0.25
step_rate = 0.1

LANES = 128
F32 = jnp.float32
BF16 = jnp.bfloat16


def split(x):
    hi = x.astype(BF16)
    return hi, (x - hi.astype(F32)).astype(BF16)


def dot(a, b):
    return jnp.dot(a, b, preferred_element_type=F32)


def dot_first(a, b):
    return lax.dot_general(a, b, (((0,), (0,)), ((), ())), preferred_element_type=F32)


def dot_last(a, b):
    return lax.dot_general(a, b, (((1,), (1,)), ((), ())), preferred_element_type=F32)


def kernel(
    n,
    ranks,
    psi_any,
    src_any,
    eigs,
    scale,
    base_any,
    stiff_any,
    perm_any,
    owner,
    slots,
    restrict_any,
    prolong_any,
    pot_any,
    adj,
    upd,
    kin,
    psi,
    node,
    idx,
    yl,
    yr,
    src,
    base,
    stiff,
    perm,
    restrict,
    prolong,
    pot,
    early,
    it,
    rsrc,
    wb,
    eg,
    edge,
    resp,
    trace_l,
    trace_r,
    dens,
    tx_l,
    tx_r,
    rx_l,
    rx_r,
    ex_tl,
    ex_tr,
    ex_l,
    ex_r,
    early_all,
    rows_all,
    own,
    mt_lo,
    mt_hi,
    tcols,
    tturn,
    packed,
    packed_in,
    fs,
    fr,
    xs,
    xr,
    es,
    er,
    ps,
    pr,
    ws,
    wr,
    ins,
):
    cells, orbs, nodes = psi.shape
    end = cells - 1
    faces = perm.shape[1]
    half = cells // 2
    prow = pot.shape[0]
    phalf = prow // 2
    coarse = pot.shape[1]
    last = nodes - LANES
    parts = nodes // LANES
    group = 8 if cells % 8 == 0 else 1
    d = lax.axis_index("dom")
    r = lax.axis_index("orb")
    barrier = pltpu.get_barrier_semaphore()
    spans = ((0, ITERS), (cells - ITERS, ITERS), (ITERS, cells - 2 * ITERS))
    src_copies = [
        pltpu.make_async_copy(src_any.at[pl.ds(a, m)], src.at[pl.ds(a, m)], ins.at[k])
        for k, (a, m) in enumerate(spans)
    ]
    psi_copy = pltpu.make_async_copy(psi_any, psi, ins.at[3])
    small = ((stiff_any, stiff), (base_any, base), (perm_any, perm), (pot_any, pot), (restrict_any, restrict), (prolong_any, prolong))
    stiff_copy, base_copy, perm_copy, pot_copy, restrict_copy, prolong_copy = [
        pltpu.make_async_copy(a, b, ins.at[4 + k]) for k, (a, b) in enumerate(small)
    ]
    for copy in (perm_copy, base_copy, src_copies[0], src_copies[1], stiff_copy, pot_copy, src_copies[2], psi_copy):
        copy.start()
    restrict_copy.start()
    prolong_copy.start()

    def greet_dom(k, carry):
        pl.semaphore_signal(barrier, inc=1, device_id={"dom": lax.rem(d + k, n)}, device_id_type=pl.DeviceIdType.MESH)
        return carry

    def greet_orb(k, carry):
        pl.semaphore_signal(barrier, inc=1, device_id={"orb": lax.rem(r + k, ranks)}, device_id_type=pl.DeviceIdType.MESH)
        return carry

    lax.fori_loop(1, n, greet_dom, 0)
    lax.fori_loop(1, ranks, greet_orb, 0)

    def send(source, target, s, t, where):
        return pltpu.make_async_remote_copy(
            src_ref=source,
            dst_ref=target,
            send_sem=s,
            recv_sem=t,
            device_id=where,
            device_id_type=pl.DeviceIdType.MESH,
        )

    right = {"dom": jnp.minimum(d + 1, n - 1)}
    left = {"dom": jnp.maximum(d - 1, 0)}
    has_right = d < n - 1
    has_left = d > 0
    f_left = send(tx_l, rx_r, fs.at[0], fr.at[0], left)
    f_right = send(tx_r, rx_l, fs.at[1], fr.at[1], right)
    x_left = send(ex_tl, ex_r, xs.at[0], xr.at[0], left)
    x_right = send(ex_tr, ex_l, xs.at[1], xr.at[1], right)

    def early_copy(k):
        return send(early, early_all.at[d], es.at[k], er.at[k], {"dom": lax.rem(d + k, n)})

    def rows_copy(k):
        return send(own, rows_all.at[d], ps.at[k], pr.at[k], {"dom": lax.rem(d + k, n)})

    def rank_copy(k):
        return send(packed, packed_in.at[k], ws.at[k], wr.at[k], {"orb": lax.rem(r + k, ranks)})

    lane = lax.broadcasted_iota(jnp.int32, (orbs, LANES), 1)
    low = lane < LANES // 2

    def turned(x, row):
        return jnp.take_along_axis(x, jnp.broadcast_to(row, (orbs, LANES)), axis=1)

    def swap(x):
        return pltpu.roll(x, LANES // 2, 1)

    def cut(b):
        return slice(b * LANES, (b + 1) * LANES)

    row0 = lax.broadcasted_iota(jnp.int32, (orbs, LANES), 0)
    column = jnp.zeros((orbs, LANES), F32)
    for o in range(orbs):
        column = jnp.where(row0 == o, relax * eigs[o], column)
    eg[...] = column
    lane1 = lax.broadcasted_iota(jnp.int32, (1, LANES), 1)
    perm_copy.wait()
    tcols[...] = jnp.zeros_like(tcols)
    tcols[:cells, :faces] = perm[...].astype(F32)
    tturn[...] = jnp.transpose(tcols[...])
    place = lax.broadcasted_iota(jnp.int32, (faces, LANES), 0).astype(F32)
    inverse = jnp.zeros((faces, LANES), F32)
    for k in range(faces):
        inverse = jnp.where(place == tturn[k : k + 1, :], float(k), inverse)
    tturn[:faces] = inverse
    tturn[faces:] = tturn[faces:] * 0.0
    inverse = jnp.transpose(tturn[...])[:cells]
    lanes = lax.broadcasted_iota(jnp.int32, (cells, LANES), 1)
    both = jnp.where(lanes < faces, inverse + faces, pltpu.roll(tcols[:cells], faces, 1))
    idx[...] = both.astype(jnp.int32)
    base_copy.wait()
    wb[...] = 1.0 - relax * base[...]

    def row_of(c):
        return idx[c : c + 1, :]

    def moved(value, product, c, b):
        return (wb[c : c + 1, cut(b)] + eg[...]) * value - (relax * scale[c]) * product

    src_copies[0].wait()
    src_copies[1].wait()
    at = list(range(ITERS)) + [cells - ITERS + s for s in range(ITERS)]
    for s, c in enumerate(at):
        edge[s] = relax * src[c].astype(F32)
        rsrc[c] = edge[s]
    stiff_copy.wait()
    for t in range(ITERS):
        count = ITERS - t
        live = list(range(count)) + list(range(2 * ITERS - count, 2 * ITERS))
        block = jnp.concatenate([edge[s] for s in live], axis=0).astype(BF16)
        if t == ITERS - 1:
            p0 = dot(block[:orbs], stiff[:, :LANES])
            p3 = dot(block[orbs:], stiff[:, last:])
            trace_l[t] = edge[0, :, :LANES] - moved(edge[0, :, :LANES], p0, 0, 0)
            s = 2 * ITERS - 1
            trace_r[t] = edge[s, :, last:] - moved(edge[s, :, last:], p3, end, parts - 1)
            break
        product = dot(block, stiff[...])
        q0, q3 = {}, {}
        for j, s in enumerate(live):
            c = at[s]
            for b in range(parts):
                value = edge[s, :, cut(b)]
                new = moved(value, product[j * orbs : (j + 1) * orbs, cut(b)], c, b)
                edge[s, :, cut(b)] = new + rsrc[c, :, cut(b)]
                if b == 0:
                    q0[s] = value - new
                if b == parts - 1:
                    q3[s] = value - new
        trace_l[t] = q0[0]
        trace_r[t] = q3[2 * ITERS - 1]
        for j in range(len(live) - 1):
            s = live[j]
            if live[j + 1] == s + 1 and s != ITERS - 1:
                y = turned(jnp.where(low, q0[s + 1], q3[s]), row_of(at[s]))
                edge[s + 1, :, :LANES] = edge[s + 1, :, :LANES] - jnp.where(low, y, 0.0)
                edge[s, :, last:] = edge[s, :, last:] - jnp.where(low, 0.0, y)
    for k in range(ITERS // 2):
        a, b = trace_l[2 * k], trace_l[2 * k + 1]
        tx_l[k * orbs : (k + 1) * orbs] = jnp.where(low, a, swap(b))
        a, b = trace_r[2 * k], trace_r[2 * k + 1]
        tx_r[k * orbs : (k + 1) * orbs] = jnp.where(low, swap(a), b)
    meta = ITERS // 2 * orbs
    for buffer, near, far, pair in ((tx_l, 0, 1, 0), (tx_r, end, end - 1, end - 1)):
        buffer[meta:] = jnp.zeros_like(buffer[meta:])
        for b in range(parts):
            buffer[meta + b : meta + b + 1] = wb[near : near + 1, cut(b)]
            buffer[meta + parts + b : meta + parts + b + 1] = wb[far : far + 1, cut(b)]
        rest = meta + 2 * parts
        buffer[rest : rest + 1] = jnp.full((1, LANES), relax * scale[near], F32)
        buffer[rest + 1 : rest + 2] = jnp.full((1, LANES), relax * scale[far], F32)
        buffer[rest + 2 : rest + 3] = row_of(pair).astype(F32)
        buffer[rest + 3 : rest + 4] = row_of(end).astype(F32)
    pot_copy.wait()
    row = jnp.zeros((1, LANES), jnp.int32)
    for c in range(cells):
        row = jnp.where(lane1 == c, owner[c] * prow + slots[c], row)
    early[:phalf] = jnp.concatenate([pot[:phalf], pot[phalf:]], axis=1)
    early[phalf:] = jnp.broadcast_to(row.astype(F32), (8, LANES))
    pl.semaphore_wait(barrier, n - 1 + ranks - 1)

    @pl.when(has_left)
    def _():
        f_left.start()

    @pl.when(has_right)
    def _():
        f_right.start()

    def send_early(k, carry):
        early_copy(k).start()
        return carry

    def start_group(g, carry):
        span = pl.ds(g * group, group)
        value = relax * src[span].astype(F32)
        rsrc[span] = value
        it[span] = value
        return carry

    src_copies[2].wait()
    lax.fori_loop(0, cells // group, start_group, 0)

    def sweep(final):
        before = None
        for g in range(cells // group):
            span = slice(g * group, (g + 1) * group)
            product = dot(it[span].reshape(group * orbs, nodes).astype(BF16), stiff[...])
            for k in range(group):
                c = g * group + k
                extra = c if c < ITERS else c - (cells - 2 * ITERS) if c >= cells - ITERS else None

                def put(c, b, value):
                    if final:
                        adj[c, :, cut(b)] = value.astype(BF16)
                        dens[c : c + 1, cut(b)] = jnp.sum(psi[c, :, cut(b)].astype(F32) * value, axis=0, keepdims=True)
                    else:
                        it[c, :, cut(b)] = value

                for b in range(parts):
                    value, source = it[c, :, cut(b)], rsrc[c, :, cut(b)]
                    new = moved(value, product[k * orbs : (k + 1) * orbs, cut(b)], c, b) + source
                    old = value + source - new
                    if final and extra is not None:
                        new = new + resp[extra, :, cut(b)]
                    if b == 0 and c > 0:
                        y = turned(jnp.where(low, old, before[0]), row_of(c - 1))
                        new = new - jnp.where(low, y, 0.0)
                        put(c - 1, parts - 1, before[1] - jnp.where(low, 0.0, y))
                    if b == parts - 1:
                        before = (old, new)
                    else:
                        put(c, b, new)
        put(end, parts - 1, before[1])

    shares = -(-(n - 1) // max(1, ITERS - 1))

    def free_sweep(t, carry):
        lax.fori_loop(jnp.minimum(n, 1 + t * shares), jnp.minimum(n, 1 + (t + 1) * shares), send_early, 0)
        sweep(False)
        return carry

    lax.fori_loop(0, ITERS - 1, free_sweep, 0)

    @pl.when(has_left)
    def _():
        f_right.wait_recv()

    @pl.when(has_right)
    def _():
        f_left.wait_recv()

    def coming(has, buffer):
        return jnp.where(has, buffer[...], 0.0)

    in_r, in_l = coming(has_right, rx_r), coming(has_left, rx_l)
    rest = meta + 2 * parts

    def near_row(buffer, at):
        return buffer[at : at + 1]

    def ghosts(buffer):
        rows = [[near_row(buffer, meta + j * parts + b) for b in range(parts)] for j in range(2)]
        return [(rows[j], near_row(buffer, rest + j)) for j in range(2)]

    def owned(c):
        return [wb[c : c + 1, cut(b)] for b in range(parts)], relax * scale[c]

    ghost_r, ghost_l = ghosts(in_r), ghosts(in_l)
    pair_r = near_row(in_r, rest + 2).astype(jnp.int32)
    pair_l = near_row(in_l, rest + 2).astype(jnp.int32)
    joint_l = near_row(in_l, rest + 3).astype(jnp.int32)
    chain_r = [(ITERS + s, owned(cells - ITERS + s)) for s in range(ITERS)] + [(2 * ITERS + j, ghost_r[j]) for j in range(2)]
    chain_l = [(2 * ITERS + 3 - j, ghost_l[1 - j]) for j in range(2)] + [(s, owned(s)) for s in range(ITERS)]
    pairs_r = [row_of(cells - ITERS + s) for s in range(ITERS)] + [pair_r]
    pairs_l = [pair_l, joint_l] + [row_of(s) for s in range(ITERS - 1)]
    sides = ((chain_r, pairs_r, ITERS - 1, has_right), (chain_l, pairs_l, 1, has_left))

    def forcing(t):
        k, odd = t // 2, t % 2
        far = in_r[k * orbs : (k + 1) * orbs]
        far = swap(far) if odd else far
        y_r = turned(jnp.where(low, far, trace_r[t]), pairs_r[ITERS - 1])
        far = in_l[k * orbs : (k + 1) * orbs]
        far = far if odd else swap(far)
        y_l = turned(jnp.where(low, trace_l[t], far), joint_l)
        return jnp.where(has_right, y_r, 0.0), jnp.where(has_left, y_l, 0.0)

    for s in range(2 * ITERS + 4):
        resp[s] = jnp.zeros((orbs, nodes), F32)
    for t in range(ITERS):
        forced = forcing(t)
        live = []
        for chain, _, joint, _ in sides:
            first, stop = max(0, joint + 1 - t), min(len(chain), joint + 1 + t)
            if t == ITERS - 1:
                first, stop = 1, ITERS + 1
            live.append(list(range(first, stop)))
        if t > 0:
            stack = [resp[chain[j][0]] for (chain, _, _, _), js in zip(sides, live) for j in js]
            product = dot(jnp.concatenate(stack, axis=0).astype(BF16), stiff[...])
        offset = 0
        for (chain, pairs, joint, _), js, push in zip(sides, live, forced):
            q0, q3 = {}, {}
            for j in js:
                s, (rows, a) = chain[j]
                for b in range(parts):
                    value = resp[s, :, cut(b)]
                    new = (rows[b] + eg[...]) * value - a * product[offset : offset + orbs, cut(b)]
                    resp[s, :, cut(b)] = new
                    if b == 0:
                        q0[j] = value - new
                    if b == parts - 1:
                        q3[j] = value - new
                offset += orbs
            zero = jnp.zeros((orbs, LANES), F32)
            for j in range(len(chain) - 1):
                if j != joint and j not in q3 and j + 1 not in q0:
                    continue
                y = zero
                if j in q3 or j + 1 in q0:
                    y = turned(jnp.where(low, q0.get(j + 1, zero), q3.get(j, zero)), pairs[j])
                if j == joint:
                    y = y + push
                a, b = chain[j][0], chain[j + 1][0]
                resp[b, :, :LANES] = resp[b, :, :LANES] - jnp.where(low, y, 0.0)
                resp[a, :, last:] = resp[a, :, last:] - jnp.where(low, 0.0, y)

    psi_copy.wait()
    sweep(True)
    restrict_copy.wait()
    d_hi, d_lo = split(dens[...])
    projected = dot_last(d_hi, restrict[...]) + dot_last(d_lo, restrict[...])
    rows = jnp.concatenate([projected[:half], projected[half:]], axis=1)
    own[...] = rows
    rows_all[d] = rows

    def send_rows(k, carry):
        rows_copy(k).start()
        return carry

    lax.fori_loop(1, n, send_rows, 0)

    def apply_group(g, carry):
        block = psi[pl.ds(g * group, group)].astype(F32).reshape(group * orbs, nodes).astype(BF16)
        product = dot(block, stiff[...])
        for k in range(group):
            c = g * group + k
            part = product[k * orbs : (k + 1) * orbs]
            kin[c] = scale[c] * part + base[pl.ds(c, 1), :] * psi[c].astype(F32)
        return carry

    groups = cells // group
    apply_group(0, 0)
    apply_group(groups - 1, 0)
    ex_tl[...] = jnp.where(low, kin[0, :, :LANES], swap(psi[0].astype(F32)[:, :LANES]))
    ex_tr[...] = jnp.where(low, swap(kin[end, :, last:]), psi[end].astype(F32)[:, last:])

    @pl.when(has_left)
    def _():
        x_left.start()

    @pl.when(has_right)
    def _():
        x_right.start()

    lax.fori_loop(1, groups - 1, apply_group, 0)
    early_all[d] = early[...]

    def wait_early(k, carry):
        early_copy(k).wait()
        return carry

    lax.fori_loop(1, n, wait_early, 0)

    tcols[...] = jnp.zeros_like(tcols)

    def take_row(e, carry):
        tcols[pl.ds(e, 1), :] = early_all[e, phalf : phalf + 1, :]
        return carry

    lax.fori_loop(0, n, take_row, 0)
    tturn[...] = jnp.transpose(tcols[...])
    def spot(e, at):
        row = early_all[e, phalf : phalf + 1, :]
        return jnp.sum(jnp.where(lane1 == at, row, 0.0), axis=1, keepdims=True)

    wanted = early_all[d, phalf : phalf + 1, :]
    wanted = jnp.where(lane1 == cells, spot(jnp.maximum(d - 1, 0), cells - 1), wanted)
    wanted = jnp.where(lane1 == cells + 1, spot(jnp.minimum(d + 1, n - 1), 0), wanted)
    wanted = jnp.where(lane1 >= prow, (d * prow + lane1 - prow).astype(F32), wanted)
    for e in range(n):
        rows_e = pl.ds(e * half, half)
        mt_lo[rows_e, :] = (tturn[:half, e : e + 1] == wanted).astype(F32)
        mt_hi[rows_e, :] = (tturn[half : 2 * half, e : e + 1] == wanted).astype(F32)
    wanted_i = wanted.astype(jnp.int32)
    slot = wanted_i % prow
    spread = (wanted_i // prow) * phalf + slot % phalf
    hit = lax.broadcasted_iota(jnp.int32, (n * phalf, LANES), 0) == spread
    table = early_all[:, :phalf, :].reshape(n * phalf, LANES)
    t_hi, t_lo = split(table)
    hit_lo = jnp.where(hit & (slot < phalf), 1.0, 0.0).astype(BF16)
    hit_hi = jnp.where(hit & (slot >= phalf), 1.0, 0.0).astype(BF16)
    pot_rows = dot_first(hit_lo, t_hi) + dot_first(hit_lo, t_lo)
    pot_rows = pot_rows + pltpu.roll(dot_first(hit_hi, t_hi) + dot_first(hit_hi, t_lo), LANES // 2, 1)

    def wait_rows(k, carry):
        rows_copy(k).wait()
        return carry

    lax.fori_loop(1, n, wait_rows, 0)
    g_hi, g_lo = split(rows_all[...].reshape(n * half, LANES))
    m_lo, m_hi = mt_lo[...].astype(BF16), mt_hi[...].astype(BF16)
    total = dot_first(m_lo, g_hi) + dot_first(m_lo, g_lo)
    total = total + pltpu.roll(dot_first(m_hi, g_hi) + dot_first(m_hi, g_lo), LANES // 2, 1)
    lane64 = lax.broadcasted_iota(jnp.int32, (prow, LANES), 1)
    mine = jnp.where(lane64 < coarse, total[:prow], pltpu.roll(total[prow:], LANES // 2, 1))
    packed[...] = mine
    for k in range(1, ranks):
        rank_copy(k).start()
    for k in range(1, ranks):
        rank_copy(k).wait()
        mine = mine + packed_in[k]
    upd[...] = pot[...] - step_rate * pltpu.roll(mine, LANES // 2, 1)[:, :coarse]
    prolong_copy.wait()
    c_hi, c_lo = split((pot_rows[:prow] - step_rate * mine)[:, :coarse])
    node[...] = dot(c_hi, prolong[...]) + dot(c_lo, prolong[...])

    yl[...] = jnp.zeros_like(yl)
    yr[...] = jnp.zeros_like(yr)

    @pl.when(has_left)
    def _():
        x_right.wait_recv()
        far = swap(ex_l[...]) + node[cells : cells + 1, last:] * ex_l[...]
        y = turned(far, rx_l[rest + 3 : rest + 4].astype(jnp.int32))
        yl[...] = jnp.where(low, y, 0.0)

    @pl.when(has_right)
    def _():
        x_left.wait_recv()
        far = ex_r[...] + node[cells + 1 : cells + 2, :LANES] * swap(ex_r[...])
        y = turned(far, row_of(end))
        yr[...] = jnp.where(low, 0.0, y)

    @pl.when(has_left)
    def _():
        x_left.wait_send()
        f_left.wait_send()

    @pl.when(has_right)
    def _():
        x_right.wait_send()
        f_right.wait_send()


def finish(
    adj,
    upd,
    kin,
    psi,
    node,
    idx,
    yl,
    yr,
    adj_out,
    upd_out,
    app_out,
    app,
    sems,
):
    cells, orbs, nodes = psi.shape
    end = cells - 1
    parts = nodes // LANES
    group = 8 if cells % 8 == 0 else 1
    groups = cells // group
    adj_copy = pltpu.make_async_copy(adj, adj_out, sems.at[groups])
    upd_copy = pltpu.make_async_copy(upd, upd_out, sems.at[groups + 1])
    adj_copy.start()
    upd_copy.start()
    low = lax.broadcasted_iota(jnp.int32, (orbs, LANES), 1) < LANES // 2
    copies = []
    before = None
    start = 0
    for g in range(groups):
        for k in range(group):
            c = g * group + k
            for b in range(parts):
                at = slice(b * LANES, (b + 1) * LANES)
                value = kin[c, :, at] + node[c : c + 1, at] * psi[c, :, at].astype(F32)
                if b == 0:
                    if c == 0:
                        new = value + yl[...]
                    else:
                        row = jnp.broadcast_to(idx[c - 1 : c, :], (orbs, LANES))
                        y = jnp.take_along_axis(jnp.where(low, value, before), row, axis=1)
                        new = value + jnp.where(low, y, 0.0)
                        app[c - 1, :, nodes - LANES :] = (before + jnp.where(low, 0.0, y)).astype(BF16)
                    app[c, :, at] = new.astype(BF16)
                elif b == parts - 1:
                    before = value
                else:
                    app[c, :, at] = value.astype(BF16)
        stop = (g + 1) * group - 1
        if g == groups - 1:
            app[end, :, nodes - LANES :] = (before + yr[...]).astype(BF16)
            stop = cells
        if stop > start:
            span = pl.ds(start, stop - start)
            copies.append(pltpu.make_async_copy(app.at[span], app_out.at[span], sems.at[g]))
            copies[-1].start()
            start = stop
    adj_copy.wait()
    upd_copy.wait()
    for copy in copies:
        copy.wait()


def local(
    n,
    ranks,
    orbitals,
    adjoint_source,
    eigenvalues,
    cell_scale,
    base_potential,
    stiffness,
    face_perm,
    restrict,
    prolong,
    owner,
    pot_slot,
    potential,
):
    cells, orbs, nodes = orbitals.shape
    prow = potential.shape[0]
    vmem = pl.BlockSpec(memory_space=pltpu.VMEM)
    smem = pl.BlockSpec(memory_space=pltpu.SMEM)
    hbm = pl.BlockSpec(memory_space=pl.ANY)
    dma = pltpu.SemaphoreType.DMA
    half = cells // 2
    face = (orbs, LANES)
    shape = orbitals.shape
    meta = -(-(2 * (nodes // LANES) + 4) // 8) * 8
    message = (ITERS // 2 * orbs + meta, LANES)
    held = 8 * orbitals.size + 4 * (prow * nodes + cells * LANES + prow * LANES + 2 * orbs * LANES)
    room = min(60 * 2**20, 64 * 2**20 - held - 2**18) // 2**15 * 2**15
    results = pl.pallas_call(
        functools.partial(kernel, n, ranks),
        out_shape=(
            pltpu.VMEM(shape, BF16),
            pltpu.VMEM(potential.shape, F32),
            pltpu.VMEM(shape, F32),
            pltpu.VMEM(shape, BF16),
            pltpu.VMEM((prow, nodes), F32),
            pltpu.VMEM((cells, LANES), jnp.int32),
            pltpu.VMEM(face, F32),
            pltpu.VMEM(face, F32),
        ),
        in_specs=[hbm, hbm, smem, smem, hbm, hbm, hbm, smem, smem, hbm, hbm, hbm],
        out_specs=(vmem,) * 8,
        scratch_shapes=[
            pltpu.VMEM(shape, BF16),
            pltpu.VMEM((cells, nodes), F32),
            pltpu.VMEM(stiffness.shape, BF16),
            pltpu.VMEM(face_perm.shape, jnp.int32),
            pltpu.VMEM(restrict.shape[::-1], BF16),
            pltpu.VMEM(prolong.shape, BF16),
            pltpu.VMEM(potential.shape, F32),
            pltpu.VMEM((prow // 2 + 8, LANES), F32),
            pltpu.VMEM(shape, F32),
            pltpu.VMEM(shape, F32),
            pltpu.VMEM((cells, nodes), F32),
            pltpu.VMEM(face, F32),
            pltpu.VMEM((2 * ITERS, orbs, nodes), F32),
            pltpu.VMEM((2 * ITERS + 4, orbs, nodes), F32),
            pltpu.VMEM((ITERS,) + face, F32),
            pltpu.VMEM((ITERS,) + face, F32),
            pltpu.VMEM((cells, nodes), F32),
            pltpu.VMEM(message, F32),
            pltpu.VMEM(message, F32),
            pltpu.VMEM(message, F32),
            pltpu.VMEM(message, F32),
            pltpu.VMEM(face, F32),
            pltpu.VMEM(face, F32),
            pltpu.VMEM(face, F32),
            pltpu.VMEM(face, F32),
            pltpu.VMEM((n, prow // 2 + 8, LANES), F32),
            pltpu.VMEM((n, half, LANES), F32),
            pltpu.VMEM((half, LANES), F32),
            pltpu.VMEM((n * half, LANES), F32),
            pltpu.VMEM((n * half, LANES), F32),
            pltpu.VMEM((LANES, LANES), F32),
            pltpu.VMEM((LANES, LANES), F32),
            pltpu.VMEM((prow, LANES), F32),
            pltpu.VMEM((ranks, prow, LANES), F32),
            dma((2,)),
            dma((2,)),
            dma((2,)),
            dma((2,)),
            dma((n,)),
            dma((n,)),
            dma((n,)),
            dma((n,)),
            dma((ranks,)),
            dma((ranks,)),
            dma((10,)),
        ],
        compiler_params=pltpu.CompilerParams(collective_id=0, has_side_effects=True, vmem_limit_bytes=room),
    )(
        orbitals,
        adjoint_source,
        eigenvalues,
        cell_scale,
        base_potential,
        stiffness,
        face_perm,
        owner[:, 0],
        pot_slot,
        restrict.T,
        prolong,
        potential,
    )
    groups = cells // (8 if cells % 8 == 0 else 1)
    return pl.pallas_call(
        finish,
        out_shape=(
            jax.ShapeDtypeStruct(shape, BF16),
            jax.ShapeDtypeStruct(potential.shape, F32),
            jax.ShapeDtypeStruct(shape, BF16),
        ),
        in_specs=[vmem] * 8,
        out_specs=(hbm, hbm, hbm),
        scratch_shapes=[pltpu.VMEM(shape, BF16), dma((groups + 2,))],
        compiler_params=pltpu.CompilerParams(vmem_limit_bytes=8 * 2**20),
    )(*results)


def solution(mesh):
    in_specs = (
        P("dom", "orb", None),
        P("dom", "orb", None),
        P("orb"),
        P("dom"),
        P("dom", None),
        P(),
        P("dom", None),
        P(),
        P(),
        P("dom", None),
        P("dom"),
        P("dom", None),
    )
    out_specs = (P("dom", "orb", None), P("dom", None), P("dom", "orb", None))
    step = functools.partial(local, mesh.shape["dom"], mesh.shape["orb"])
    return jax.shard_map(step, mesh=mesh, in_specs=in_specs, out_specs=out_specs, check_vma=False)
```

```python
import functools

import jax
import jax.numpy as jnp
from jax import lax
from jax.experimental import pallas as pl
from jax.experimental.pallas import tpu as pltpu
from jax.sharding import PartitionSpec as P

ITERS = 4


relax = 0.25
step_rate = 0.1

LANES = 128
F32 = jnp.float32
BF16 = jnp.bfloat16


def split(x):
    hi = x.astype(BF16)
    return hi, (x - hi.astype(F32)).astype(BF16)


def dot(a, b):
    return jnp.dot(a, b, preferred_element_type=F32)


def dot_first(a, b):
    return lax.dot_general(a, b, (((0,), (0,)), ((), ())), preferred_element_type=F32)


def dot_last(a, b):
    return lax.dot_general(a, b, (((1,), (1,)), ((), ())), preferred_element_type=F32)


def kernel(
    n,
    ranks,
    psi_any,
    src_any,
    eigs_any,
    scale_any,
    base_any,
    stiff_any,
    perm_any,
    owner_any,
    slots_any,
    restrict_any,
    prolong_any,
    pot_any,
    adj,
    upd,
    kin,
    psi,
    node,
    idx,
    yl,
    yr,
    eigs,
    scale,
    owner,
    slots,
    src,
    base,
    stiff,
    perm,
    restrict,
    prolong,
    pot,
    early,
    it,
    rsrc,
    itb,
    wb,
    eg,
    edge,
    resp,
    trace_l,
    trace_r,
    dens,
    tx_l,
    tx_r,
    rx_l,
    rx_r,
    ex_tl,
    ex_tr,
    ex_l,
    ex_r,
    early_all,
    rows_all,
    own,
    mt_lo,
    mt_hi,
    tcols,
    tturn,
    packed,
    packed_in,
    fs,
    fr,
    xs,
    xr,
    es,
    er,
    ps,
    pr,
    ws,
    wr,
    ins,
):
    cells, orbs, nodes = psi.shape
    end = cells - 1
    faces = perm.shape[1]
    half = cells // 2
    prow = pot.shape[0]
    phalf = prow // 2
    coarse = pot.shape[1]
    last = nodes - LANES
    parts = nodes // LANES
    group = 8 if cells % 8 == 0 else 1
    d = lax.axis_index("dom")
    r = lax.axis_index("orb")
    barrier = pltpu.get_barrier_semaphore()
    spans = ((0, ITERS), (cells - ITERS, ITERS), (ITERS, cells - 2 * ITERS))
    src_copies = [
        pltpu.make_async_copy(src_any.at[pl.ds(a, m)], src.at[pl.ds(a, m)], ins.at[k])
        for k, (a, m) in enumerate(spans)
    ]
    psi_copy = pltpu.make_async_copy(psi_any, psi, ins.at[3])
    small = ((stiff_any, stiff), (base_any, base), (perm_any, perm), (pot_any, pot), (restrict_any, restrict), (prolong_any, prolong))
    stiff_copy, base_copy, perm_copy, pot_copy, restrict_copy, prolong_copy = [
        pltpu.make_async_copy(a, b, ins.at[4 + k]) for k, (a, b) in enumerate(small)
    ]
    scalar = ((eigs_any, eigs), (scale_any, scale), (owner_any, owner), (slots_any, slots))
    scalar_copies = [pltpu.make_async_copy(a, b, ins.at[10 + k]) for k, (a, b) in enumerate(scalar)]
    for copy in scalar_copies:
        copy.start()
    for copy in (perm_copy, base_copy, src_copies[0], src_copies[1], stiff_copy, pot_copy, src_copies[2], psi_copy):
        copy.start()
    restrict_copy.start()
    prolong_copy.start()

    def greet_dom(k, carry):
        pl.semaphore_signal(barrier, inc=1, device_id={"dom": lax.rem(d + k, n)}, device_id_type=pl.DeviceIdType.MESH)
        return carry

    def greet_orb(k, carry):
        pl.semaphore_signal(barrier, inc=1, device_id={"orb": lax.rem(r + k, ranks)}, device_id_type=pl.DeviceIdType.MESH)
        return carry

    lax.fori_loop(1, n, greet_dom, 0)
    lax.fori_loop(1, ranks, greet_orb, 0)

    def send(source, target, s, t, where):
        return pltpu.make_async_remote_copy(
            src_ref=source,
            dst_ref=target,
            send_sem=s,
            recv_sem=t,
            device_id=where,
            device_id_type=pl.DeviceIdType.MESH,
        )

    right = {"dom": jnp.minimum(d + 1, n - 1)}
    left = {"dom": jnp.maximum(d - 1, 0)}
    has_right = d < n - 1
    has_left = d > 0
    f_left = send(tx_l, rx_r, fs.at[0], fr.at[0], left)
    f_right = send(tx_r, rx_l, fs.at[1], fr.at[1], right)
    x_left = send(ex_tl, ex_r, xs.at[0], xr.at[0], left)
    x_right = send(ex_tr, ex_l, xs.at[1], xr.at[1], right)

    def early_copy(k):
        return send(early, early_all.at[d], es.at[k], er.at[k], {"dom": lax.rem(d + k, n)})

    def rows_copy(k):
        return send(own, rows_all.at[d], ps.at[k], pr.at[k], {"dom": lax.rem(d + k, n)})

    def rank_copy(k):
        return send(packed, packed_in.at[k], ws.at[k], wr.at[k], {"orb": lax.rem(r + k, ranks)})

    lane = lax.broadcasted_iota(jnp.int32, (orbs, LANES), 1)
    low = lane < LANES // 2

    def turned(x, row):
        return jnp.take_along_axis(x, jnp.broadcast_to(row, (orbs, LANES)), axis=1)

    def swap(x):
        return pltpu.roll(x, LANES // 2, 1)

    def cut(b):
        return slice(b * LANES, (b + 1) * LANES)

    for copy in scalar_copies:
        copy.wait()
    row0 = lax.broadcasted_iota(jnp.int32, (orbs, LANES), 0)
    column = jnp.zeros((orbs, LANES), F32)
    for o in range(orbs):
        column = jnp.where(row0 == o, relax * eigs[o], column)
    eg[...] = column
    lane1 = lax.broadcasted_iota(jnp.int32, (1, LANES), 1)
    perm_copy.wait()
    tcols[...] = jnp.zeros_like(tcols)
    tcols[:cells, :faces] = perm[...].astype(F32)
    tturn[...] = jnp.transpose(tcols[...])
    place = lax.broadcasted_iota(jnp.int32, (faces, LANES), 0).astype(F32)
    inverse = jnp.zeros((faces, LANES), F32)
    for k in range(faces):
        inverse = jnp.where(place == tturn[k : k + 1, :], float(k), inverse)
    tturn[:faces] = inverse
    tturn[faces:] = tturn[faces:] * 0.0
    inverse = jnp.transpose(tturn[...])[:cells]
    lanes = lax.broadcasted_iota(jnp.int32, (cells, LANES), 1)
    both = jnp.where(lanes < faces, inverse + faces, pltpu.roll(tcols[:cells], faces, 1))
    idx[...] = both.astype(jnp.int32)
    base_copy.wait()
    wb[...] = 1.0 - relax * base[...]

    def row_of(c):
        return idx[c : c + 1, :]

    def moved(value, product, c, b):
        return (wb[c : c + 1, cut(b)] + eg[...]) * value - (relax * scale[c]) * product

    src_copies[0].wait()
    src_copies[1].wait()
    at = list(range(ITERS)) + [cells - ITERS + s for s in range(ITERS)]
    for s, c in enumerate(at):
        edge[s] = relax * src[c].astype(F32)
        rsrc[c] = edge[s]
    stiff_copy.wait()
    for t in range(ITERS):
        count = ITERS - t
        live = list(range(count)) + list(range(2 * ITERS - count, 2 * ITERS))
        block = jnp.concatenate([edge[s] for s in live], axis=0).astype(BF16)
        if t == ITERS - 1:
            p0 = dot(block[:orbs], stiff[:, :LANES])
            p3 = dot(block[orbs:], stiff[:, last:])
            trace_l[t] = edge[0, :, :LANES] - moved(edge[0, :, :LANES], p0, 0, 0)
            s = 2 * ITERS - 1
            trace_r[t] = edge[s, :, last:] - moved(edge[s, :, last:], p3, end, parts - 1)
            break
        product = dot(block, stiff[...])
        q0, q3 = {}, {}
        for j, s in enumerate(live):
            c = at[s]
            for b in range(parts):
                value = edge[s, :, cut(b)]
                new = moved(value, product[j * orbs : (j + 1) * orbs, cut(b)], c, b)
                edge[s, :, cut(b)] = new + rsrc[c, :, cut(b)]
                if b == 0:
                    q0[s] = value - new
                if b == parts - 1:
                    q3[s] = value - new
        trace_l[t] = q0[0]
        trace_r[t] = q3[2 * ITERS - 1]
        for j in range(len(live) - 1):
            s = live[j]
            if live[j + 1] == s + 1 and s != ITERS - 1:
                y = turned(jnp.where(low, q0[s + 1], q3[s]), row_of(at[s]))
                edge[s + 1, :, :LANES] = edge[s + 1, :, :LANES] - jnp.where(low, y, 0.0)
                edge[s, :, last:] = edge[s, :, last:] - jnp.where(low, 0.0, y)
    for k in range(ITERS // 2):
        a, b = trace_l[2 * k], trace_l[2 * k + 1]
        tx_l[k * orbs : (k + 1) * orbs] = jnp.where(low, a, swap(b))
        a, b = trace_r[2 * k], trace_r[2 * k + 1]
        tx_r[k * orbs : (k + 1) * orbs] = jnp.where(low, swap(a), b)
    meta = ITERS // 2 * orbs
    for buffer, near, far, pair in ((tx_l, 0, 1, 0), (tx_r, end, end - 1, end - 1)):
        buffer[meta:] = jnp.zeros_like(buffer[meta:])
        for b in range(parts):
            buffer[meta + b : meta + b + 1] = wb[near : near + 1, cut(b)]
            buffer[meta + parts + b : meta + parts + b + 1] = wb[far : far + 1, cut(b)]
        rest = meta + 2 * parts
        buffer[rest : rest + 1] = jnp.full((1, LANES), relax * scale[near], F32)
        buffer[rest + 1 : rest + 2] = jnp.full((1, LANES), relax * scale[far], F32)
        buffer[rest + 2 : rest + 3] = row_of(pair).astype(F32)
        buffer[rest + 3 : rest + 4] = row_of(end).astype(F32)
    pot_copy.wait()
    row = jnp.zeros((1, LANES), jnp.int32)
    for c in range(cells):
        row = jnp.where(lane1 == c, owner[c] * prow + slots[c], row)
    early[:phalf] = jnp.concatenate([pot[:phalf], pot[phalf:]], axis=1)
    early[phalf:] = jnp.broadcast_to(row.astype(F32), (8, LANES))
    pl.semaphore_wait(barrier, n - 1 + ranks - 1)

    @pl.when(has_left)
    def _():
        f_left.start()

    @pl.when(has_right)
    def _():
        f_right.start()

    def send_early(k, carry):
        early_copy(k).start()
        return carry

    def start_group(g, carry):
        span = pl.ds(g * group, group)
        value = relax * src[span].astype(F32)
        rsrc[span] = value
        it[span] = value
        itb[span] = value.astype(BF16)
        return carry

    src_copies[2].wait()
    lax.fori_loop(0, cells // group, start_group, 0)

    def stacked(buffer, span):
        if orbs % 16:
            return buffer[span].astype(F32).reshape(group * orbs, nodes).astype(BF16)
        return buffer[span].reshape(group * orbs, nodes)

    def sweep(final):
        before = None
        shift = eg[...]
        for g in range(cells // group):
            span = slice(g * group, (g + 1) * group)
            product = dot(stacked(itb, span), stiff[...])
            for k in range(group):
                c = g * group + k
                extra = c if c < ITERS else c - (cells - 2 * ITERS) if c >= cells - ITERS else None

                def put(c, b, value):
                    if final:
                        adj[c, :, cut(b)] = value.astype(BF16)
                        dens[c : c + 1, cut(b)] = jnp.sum(psi[c, :, cut(b)].astype(F32) * value, axis=0, keepdims=True)
                    else:
                        it[c, :, cut(b)] = value
                        itb[c, :, cut(b)] = value.astype(BF16)

                for b in range(parts):
                    value, source = it[c, :, cut(b)], rsrc[c, :, cut(b)]
                    kept = (wb[c : c + 1, cut(b)] + shift) * value
                    new = kept - (relax * scale[c]) * product[k * orbs : (k + 1) * orbs, cut(b)] + source
                    old = value + source - new
                    if final and extra is not None:
                        new = new + resp[extra, :, cut(b)]
                    if b == 0 and c > 0:
                        y = turned(jnp.where(low, old, before[0]), row_of(c - 1))
                        new = new - jnp.where(low, y, 0.0)
                        put(c - 1, parts - 1, before[1] - jnp.where(low, 0.0, y))
                    if b == parts - 1:
                        before = (old, new)
                    else:
                        put(c, b, new)
        put(end, parts - 1, before[1])

    shares = -(-(n - 1) // max(1, ITERS - 1))

    def free_sweep(t, carry):
        lax.fori_loop(jnp.minimum(n, 1 + t * shares), jnp.minimum(n, 1 + (t + 1) * shares), send_early, 0)
        sweep(False)
        return carry

    lax.fori_loop(0, ITERS - 1, free_sweep, 0)

    for copy in (psi_copy, restrict_copy, prolong_copy):
        copy.wait()

    @pl.when(has_left)
    def _():
        f_right.wait_recv()

    @pl.when(has_right)
    def _():
        f_left.wait_recv()

    def coming(has, buffer):
        return jnp.where(has, buffer[...], 0.0)

    in_r, in_l = coming(has_right, rx_r), coming(has_left, rx_l)
    rest = meta + 2 * parts

    def near_row(buffer, at):
        return buffer[at : at + 1]

    def ghosts(buffer):
        rows = [[near_row(buffer, meta + j * parts + b) for b in range(parts)] for j in range(2)]
        return [(rows[j], near_row(buffer, rest + j)) for j in range(2)]

    def owned(c):
        return [wb[c : c + 1, cut(b)] for b in range(parts)], relax * scale[c]

    ghost_r, ghost_l = ghosts(in_r), ghosts(in_l)
    pair_r = near_row(in_r, rest + 2).astype(jnp.int32)
    pair_l = near_row(in_l, rest + 2).astype(jnp.int32)
    joint_l = near_row(in_l, rest + 3).astype(jnp.int32)
    chain_r = [(ITERS + s, owned(cells - ITERS + s)) for s in range(ITERS)] + [(2 * ITERS + j, ghost_r[j]) for j in range(2)]
    chain_l = [(2 * ITERS + 3 - j, ghost_l[1 - j]) for j in range(2)] + [(s, owned(s)) for s in range(ITERS)]
    pairs_r = [row_of(cells - ITERS + s) for s in range(ITERS)] + [pair_r]
    pairs_l = [pair_l, joint_l] + [row_of(s) for s in range(ITERS - 1)]
    sides = ((chain_r, pairs_r, ITERS - 1, has_right), (chain_l, pairs_l, 1, has_left))

    def forcing(t):
        k, odd = t // 2, t % 2
        far = in_r[k * orbs : (k + 1) * orbs]
        far = swap(far) if odd else far
        y_r = turned(jnp.where(low, far, trace_r[t]), pairs_r[ITERS - 1])
        far = in_l[k * orbs : (k + 1) * orbs]
        far = far if odd else swap(far)
        y_l = turned(jnp.where(low, trace_l[t], far), joint_l)
        return jnp.where(has_right, y_r, 0.0), jnp.where(has_left, y_l, 0.0)

    for s in range(2 * ITERS + 4):
        resp[s] = jnp.zeros((orbs, nodes), F32)
    for t in range(ITERS):
        forced = forcing(t)
        live = []
        for chain, _, joint, _ in sides:
            first, stop = max(0, joint + 1 - t), min(len(chain), joint + 1 + t)
            if t == ITERS - 1:
                first, stop = 1, ITERS + 1
            live.append(list(range(first, stop)))
        if t > 0:
            stack = [resp[chain[j][0]] for (chain, _, _, _), js in zip(sides, live) for j in js]
            product = dot(jnp.concatenate(stack, axis=0).astype(BF16), stiff[...])
        offset = 0
        for (chain, pairs, joint, _), js, push in zip(sides, live, forced):
            q0, q3 = {}, {}
            for j in js:
                s, (rows, a) = chain[j]
                for b in range(parts):
                    value = resp[s, :, cut(b)]
                    new = (rows[b] + eg[...]) * value - a * product[offset : offset + orbs, cut(b)]
                    resp[s, :, cut(b)] = new
                    if b == 0:
                        q0[j] = value - new
                    if b == parts - 1:
                        q3[j] = value - new
                offset += orbs
            zero = jnp.zeros((orbs, LANES), F32)
            for j in range(len(chain) - 1):
                if j != joint and j not in q3 and j + 1 not in q0:
                    continue
                y = zero
                if j in q3 or j + 1 in q0:
                    y = turned(jnp.where(low, q0.get(j + 1, zero), q3.get(j, zero)), pairs[j])
                if j == joint:
                    y = y + push
                a, b = chain[j][0], chain[j + 1][0]
                resp[b, :, :LANES] = resp[b, :, :LANES] - jnp.where(low, y, 0.0)
                resp[a, :, last:] = resp[a, :, last:] - jnp.where(low, 0.0, y)

    sweep(True)
    d_hi, d_lo = split(dens[...])
    projected = dot_last(d_hi, restrict[...]) + dot_last(d_lo, restrict[...])
    rows = jnp.concatenate([projected[:half], projected[half:]], axis=1)
    own[...] = rows
    rows_all[d] = rows

    def send_rows(k, carry):
        rows_copy(k).start()
        return carry

    lax.fori_loop(1, n, send_rows, 0)

    def apply_group(g, carry):
        block = psi[pl.ds(g * group, group)].astype(F32).reshape(group * orbs, nodes).astype(BF16)
        product = dot(block, stiff[...])
        for k in range(group):
            c = g * group + k
            part = product[k * orbs : (k + 1) * orbs]
            kin[c] = scale[c] * part + base[pl.ds(c, 1), :] * psi[c].astype(F32)
        return carry

    groups = cells // group
    apply_group(0, 0)
    apply_group(groups - 1, 0)
    ex_tl[...] = jnp.where(low, kin[0, :, :LANES], swap(psi[0].astype(F32)[:, :LANES]))
    ex_tr[...] = jnp.where(low, swap(kin[end, :, last:]), psi[end].astype(F32)[:, last:])

    @pl.when(has_left)
    def _():
        x_left.start()

    @pl.when(has_right)
    def _():
        x_right.start()

    lax.fori_loop(1, groups - 1, apply_group, 0)
    early_all[d] = early[...]

    def wait_early(k, carry):
        early_copy(k).wait()
        return carry

    lax.fori_loop(1, n, wait_early, 0)

    tcols[...] = jnp.zeros_like(tcols)

    def take_row(e, carry):
        tcols[pl.ds(e, 1), :] = early_all[e, phalf : phalf + 1, :]
        return carry

    lax.fori_loop(0, n, take_row, 0)
    tturn[...] = jnp.transpose(tcols[...])
    def spot(e, at):
        row = early_all[e, phalf : phalf + 1, :]
        return jnp.sum(jnp.where(lane1 == at, row, 0.0), axis=1, keepdims=True)

    wanted = early_all[d, phalf : phalf + 1, :]
    wanted = jnp.where(lane1 == cells, spot(jnp.maximum(d - 1, 0), cells - 1), wanted)
    wanted = jnp.where(lane1 == cells + 1, spot(jnp.minimum(d + 1, n - 1), 0), wanted)
    wanted = jnp.where(lane1 >= prow, (d * prow + lane1 - prow).astype(F32), wanted)
    for e in range(n):
        rows_e = pl.ds(e * half, half)
        mt_lo[rows_e, :] = (tturn[:half, e : e + 1] == wanted).astype(F32)
        mt_hi[rows_e, :] = (tturn[half : 2 * half, e : e + 1] == wanted).astype(F32)
    wanted_i = wanted.astype(jnp.int32)
    slot = wanted_i % prow
    spread = (wanted_i // prow) * phalf + slot % phalf
    hit = lax.broadcasted_iota(jnp.int32, (n * phalf, LANES), 0) == spread
    table = early_all[:, :phalf, :].reshape(n * phalf, LANES)
    t_hi, t_lo = split(table)
    hit_lo = jnp.where(hit & (slot < phalf), 1.0, 0.0).astype(BF16)
    hit_hi = jnp.where(hit & (slot >= phalf), 1.0, 0.0).astype(BF16)
    pot_rows = dot_first(hit_lo, t_hi) + dot_first(hit_lo, t_lo)
    pot_rows = pot_rows + pltpu.roll(dot_first(hit_hi, t_hi) + dot_first(hit_hi, t_lo), LANES // 2, 1)

    def wait_rows(k, carry):
        rows_copy(k).wait()
        return carry

    lax.fori_loop(1, n, wait_rows, 0)
    g_hi, g_lo = split(rows_all[...].reshape(n * half, LANES))
    m_lo, m_hi = mt_lo[...].astype(BF16), mt_hi[...].astype(BF16)
    total = dot_first(m_lo, g_hi) + dot_first(m_lo, g_lo)
    total = total + pltpu.roll(dot_first(m_hi, g_hi) + dot_first(m_hi, g_lo), LANES // 2, 1)
    lane64 = lax.broadcasted_iota(jnp.int32, (prow, LANES), 1)
    mine = jnp.where(lane64 < coarse, total[:prow], pltpu.roll(total[prow:], LANES // 2, 1))
    packed[...] = mine
    for k in range(1, ranks):
        rank_copy(k).start()
    for k in range(1, ranks):
        rank_copy(k).wait()
        mine = mine + packed_in[k]
    upd[...] = pot[...] - step_rate * pltpu.roll(mine, LANES // 2, 1)[:, :coarse]
    c_hi, c_lo = split((pot_rows[:prow] - step_rate * mine)[:, :coarse])
    node[...] = dot(c_hi, prolong[...]) + dot(c_lo, prolong[...])

    yl[...] = jnp.zeros_like(yl)
    yr[...] = jnp.zeros_like(yr)

    @pl.when(has_left)
    def _():
        x_right.wait_recv()
        far = swap(ex_l[...]) + node[cells : cells + 1, last:] * ex_l[...]
        y = turned(far, rx_l[rest + 3 : rest + 4].astype(jnp.int32))
        yl[...] = jnp.where(low, y, 0.0)

    @pl.when(has_right)
    def _():
        x_left.wait_recv()
        far = ex_r[...] + node[cells + 1 : cells + 2, :LANES] * swap(ex_r[...])
        y = turned(far, row_of(end))
        yr[...] = jnp.where(low, 0.0, y)

    @pl.when(has_left)
    def _():
        x_left.wait_send()
        f_left.wait_send()

    @pl.when(has_right)
    def _():
        x_right.wait_send()
        f_right.wait_send()


def finish(
    adj,
    upd,
    kin,
    psi,
    node,
    idx,
    yl,
    yr,
    adj_out,
    upd_out,
    app_out,
    app,
    sems,
):
    cells, orbs, nodes = psi.shape
    end = cells - 1
    parts = nodes // LANES
    group = 8 if cells % 8 == 0 else 1
    groups = cells // group
    adj_copy = pltpu.make_async_copy(adj, adj_out, sems.at[groups])
    upd_copy = pltpu.make_async_copy(upd, upd_out, sems.at[groups + 1])
    adj_copy.start()
    upd_copy.start()
    low = lax.broadcasted_iota(jnp.int32, (orbs, LANES), 1) < LANES // 2
    copies = []
    before = None
    start = 0
    for g in range(groups):
        for k in range(group):
            c = g * group + k
            for b in range(parts):
                at = slice(b * LANES, (b + 1) * LANES)
                value = kin[c, :, at] + node[c : c + 1, at] * psi[c, :, at].astype(F32)
                if b == 0:
                    if c == 0:
                        new = value + yl[...]
                    else:
                        row = jnp.broadcast_to(idx[c - 1 : c, :], (orbs, LANES))
                        y = jnp.take_along_axis(jnp.where(low, value, before), row, axis=1)
                        new = value + jnp.where(low, y, 0.0)
                        app[c - 1, :, nodes - LANES :] = (before + jnp.where(low, 0.0, y)).astype(BF16)
                    app[c, :, at] = new.astype(BF16)
                elif b == parts - 1:
                    before = value
                else:
                    app[c, :, at] = value.astype(BF16)
        stop = (g + 1) * group - 1
        if g == groups - 1:
            app[end, :, nodes - LANES :] = (before + yr[...]).astype(BF16)
            stop = cells
        if stop > start:
            span = pl.ds(start, stop - start)
            copies.append(pltpu.make_async_copy(app.at[span], app_out.at[span], sems.at[g]))
            copies[-1].start()
            start = stop
    adj_copy.wait()
    upd_copy.wait()
    for copy in copies:
        copy.wait()


def local(
    n,
    ranks,
    orbitals,
    adjoint_source,
    eigenvalues,
    cell_scale,
    base_potential,
    stiffness,
    face_perm,
    restrict,
    prolong,
    owner,
    pot_slot,
    potential,
):
    cells, orbs, nodes = orbitals.shape
    prow = potential.shape[0]
    vmem = pl.BlockSpec(memory_space=pltpu.VMEM)
    hbm = pl.BlockSpec(memory_space=pl.ANY)
    dma = pltpu.SemaphoreType.DMA
    half = cells // 2
    face = (orbs, LANES)
    shape = orbitals.shape
    meta = -(-(2 * (nodes // LANES) + 4) // 8) * 8
    message = (ITERS // 2 * orbs + meta, LANES)
    held = 8 * orbitals.size + 4 * (prow * nodes + cells * LANES + prow * LANES + 2 * orbs * LANES)
    room = min(60 * 2**20, 64 * 2**20 - held - 2**18) // 2**15 * 2**15
    results = pl.pallas_call(
        functools.partial(kernel, n, ranks),
        out_shape=(
            pltpu.VMEM(shape, BF16),
            pltpu.VMEM(potential.shape, F32),
            pltpu.VMEM(shape, F32),
            pltpu.VMEM(shape, BF16),
            pltpu.VMEM((prow, nodes), F32),
            pltpu.VMEM((cells, LANES), jnp.int32),
            pltpu.VMEM(face, F32),
            pltpu.VMEM(face, F32),
        ),
        in_specs=[hbm] * 12,
        out_specs=(vmem,) * 8,
        scratch_shapes=[
            pltpu.SMEM((orbs,), F32),
            pltpu.SMEM((cells,), F32),
            pltpu.SMEM((cells,), jnp.int32),
            pltpu.SMEM((cells,), jnp.int32),
            pltpu.VMEM(shape, BF16),
            pltpu.VMEM((cells, nodes), F32),
            pltpu.VMEM(stiffness.shape, BF16),
            pltpu.VMEM(face_perm.shape, jnp.int32),
            pltpu.VMEM(restrict.shape[::-1], BF16),
            pltpu.VMEM(prolong.shape, BF16),
            pltpu.VMEM(potential.shape, F32),
            pltpu.VMEM((prow // 2 + 8, LANES), F32),
            pltpu.VMEM(shape, F32),
            pltpu.VMEM(shape, F32),
            pltpu.VMEM(shape, BF16),
            pltpu.VMEM((cells, nodes), F32),
            pltpu.VMEM(face, F32),
            pltpu.VMEM((2 * ITERS, orbs, nodes), F32),
            pltpu.VMEM((2 * ITERS + 4, orbs, nodes), F32),
            pltpu.VMEM((ITERS,) + face, F32),
            pltpu.VMEM((ITERS,) + face, F32),
            pltpu.VMEM((cells, nodes), F32),
            pltpu.VMEM(message, F32),
            pltpu.VMEM(message, F32),
            pltpu.VMEM(message, F32),
            pltpu.VMEM(message, F32),
            pltpu.VMEM(face, F32),
            pltpu.VMEM(face, F32),
            pltpu.VMEM(face, F32),
            pltpu.VMEM(face, F32),
            pltpu.VMEM((n, prow // 2 + 8, LANES), F32),
            pltpu.VMEM((n, half, LANES), F32),
            pltpu.VMEM((half, LANES), F32),
            pltpu.VMEM((n * half, LANES), F32),
            pltpu.VMEM((n * half, LANES), F32),
            pltpu.VMEM((LANES, LANES), F32),
            pltpu.VMEM((LANES, LANES), F32),
            pltpu.VMEM((prow, LANES), F32),
            pltpu.VMEM((ranks, prow, LANES), F32),
            dma((2,)),
            dma((2,)),
            dma((2,)),
            dma((2,)),
            dma((n,)),
            dma((n,)),
            dma((n,)),
            dma((n,)),
            dma((ranks,)),
            dma((ranks,)),
            dma((14,)),
        ],
        compiler_params=pltpu.CompilerParams(collective_id=0, has_side_effects=True, vmem_limit_bytes=room),
    )(
        orbitals,
        adjoint_source,
        eigenvalues,
        cell_scale,
        base_potential,
        stiffness,
        face_perm,
        owner[:, 0],
        pot_slot,
        restrict.T,
        prolong,
        potential,
    )
    groups = cells // (8 if cells % 8 == 0 else 1)
    return pl.pallas_call(
        finish,
        out_shape=(
            jax.ShapeDtypeStruct(shape, BF16),
            jax.ShapeDtypeStruct(potential.shape, F32),
            jax.ShapeDtypeStruct(shape, BF16),
        ),
        in_specs=[vmem] * 8,
        out_specs=(hbm, hbm, hbm),
        scratch_shapes=[pltpu.VMEM(shape, BF16), dma((groups + 2,))],
        compiler_params=pltpu.CompilerParams(vmem_limit_bytes=8 * 2**20),
    )(*results)


def solution(mesh):
    in_specs = (
        P("dom", "orb", None),
        P("dom", "orb", None),
        P("orb"),
        P("dom"),
        P("dom", None),
        P(),
        P("dom", None),
        P(),
        P(),
        P("dom", None),
        P("dom"),
        P("dom", None),
    )
    out_specs = (P("dom", "orb", None), P("dom", None), P("dom", "orb", None))
    step = functools.partial(local, mesh.shape["dom"], mesh.shape["orb"])
    return jax.shard_map(step, mesh=mesh, in_specs=in_specs, out_specs=out_specs, check_vma=False)
```

```python
import functools

import jax
import jax.numpy as jnp
from jax import lax
from jax.experimental import pallas as pl
from jax.experimental.pallas import tpu as pltpu
from jax.sharding import PartitionSpec as P

ITERS = 4


relax = 0.25
step_rate = 0.1

LANES = 128
F32 = jnp.float32
BF16 = jnp.bfloat16


def split(x):
    hi = x.astype(BF16)
    return hi, (x - hi.astype(F32)).astype(BF16)


def dot(a, b):
    return jnp.dot(a, b, preferred_element_type=F32)


def dot_first(a, b):
    return lax.dot_general(a, b, (((0,), (0,)), ((), ())), preferred_element_type=F32)


def dot_last(a, b):
    return lax.dot_general(a, b, (((1,), (1,)), ((), ())), preferred_element_type=F32)


def kernel(
    n,
    ranks,
    psi_any,
    src_any,
    eigs_any,
    scale_any,
    base_any,
    stiff_any,
    perm_any,
    owner_any,
    slots_any,
    restrict_any,
    prolong_any,
    pot_any,
    adj,
    upd,
    kin,
    psi,
    node,
    idx,
    yl,
    yr,
    eigs,
    scale,
    owner,
    slots,
    src,
    base,
    stiff,
    perm,
    restrict,
    prolong,
    pot,
    early,
    it,
    itb,
    wb,
    eg,
    edge,
    resp,
    trace_l,
    trace_r,
    dens,
    tx_l,
    tx_r,
    rx_l,
    rx_r,
    ex_tl,
    ex_tr,
    ex_l,
    ex_r,
    early_all,
    rows_all,
    own,
    mt_lo,
    mt_hi,
    tcols,
    tturn,
    packed,
    packed_in,
    fs,
    fr,
    xs,
    xr,
    es,
    er,
    ps,
    pr,
    ws,
    wr,
    ins,
):
    cells, orbs, nodes = psi.shape
    end = cells - 1
    faces = perm.shape[1]
    half = cells // 2
    prow = pot.shape[0]
    phalf = prow // 2
    coarse = pot.shape[1]
    last = nodes - LANES
    parts = nodes // LANES
    group = 8 if cells % 8 == 0 else 1
    d = lax.axis_index("dom")
    r = lax.axis_index("orb")
    barrier = pltpu.get_barrier_semaphore()
    spans = ((0, ITERS), (cells - ITERS, ITERS), (ITERS, cells - 2 * ITERS))
    src_copies = [
        pltpu.make_async_copy(src_any.at[pl.ds(a, m)], src.at[pl.ds(a, m)], ins.at[k])
        for k, (a, m) in enumerate(spans)
    ]
    psi_copy = pltpu.make_async_copy(psi_any, psi, ins.at[3])
    small = ((stiff_any, stiff), (base_any, base), (perm_any, perm), (pot_any, pot), (restrict_any, restrict), (prolong_any, prolong))
    stiff_copy, base_copy, perm_copy, pot_copy, restrict_copy, prolong_copy = [
        pltpu.make_async_copy(a, b, ins.at[4 + k]) for k, (a, b) in enumerate(small)
    ]
    scalar = ((eigs_any, eigs), (scale_any, scale), (owner_any, owner), (slots_any, slots))
    scalar_copies = [pltpu.make_async_copy(a, b, ins.at[10 + k]) for k, (a, b) in enumerate(scalar)]
    for copy in scalar_copies:
        copy.start()
    for copy in (perm_copy, base_copy, src_copies[0], src_copies[1], stiff_copy, pot_copy, src_copies[2], psi_copy):
        copy.start()
    restrict_copy.start()
    prolong_copy.start()

    def greet_dom(k, carry):
        pl.semaphore_signal(barrier, inc=1, device_id={"dom": lax.rem(d + k, n)}, device_id_type=pl.DeviceIdType.MESH)
        return carry

    def greet_orb(k, carry):
        pl.semaphore_signal(barrier, inc=1, device_id={"orb": lax.rem(r + k, ranks)}, device_id_type=pl.DeviceIdType.MESH)
        return carry

    lax.fori_loop(1, n, greet_dom, 0)
    lax.fori_loop(1, ranks, greet_orb, 0)

    def send(source, target, s, t, where):
        return pltpu.make_async_remote_copy(
            src_ref=source,
            dst_ref=target,
            send_sem=s,
            recv_sem=t,
            device_id=where,
            device_id_type=pl.DeviceIdType.MESH,
        )

    right = {"dom": jnp.minimum(d + 1, n - 1)}
    left = {"dom": jnp.maximum(d - 1, 0)}
    has_right = d < n - 1
    has_left = d > 0
    f_left = send(tx_l, rx_r, fs.at[0], fr.at[0], left)
    f_right = send(tx_r, rx_l, fs.at[1], fr.at[1], right)
    x_left = send(ex_tl, ex_r, xs.at[0], xr.at[0], left)
    x_right = send(ex_tr, ex_l, xs.at[1], xr.at[1], right)

    def early_copy(k):
        return send(early, early_all.at[d], es.at[k], er.at[k], {"dom": lax.rem(d + k, n)})

    def rows_copy(k):
        return send(own, rows_all.at[d], ps.at[k], pr.at[k], {"dom": lax.rem(d + k, n)})

    def rank_copy(k):
        return send(packed, packed_in.at[k], ws.at[k], wr.at[k], {"orb": lax.rem(r + k, ranks)})

    lane = lax.broadcasted_iota(jnp.int32, (orbs, LANES), 1)
    low = lane < LANES // 2

    def turned(x, row):
        return jnp.take_along_axis(x, jnp.broadcast_to(row, (orbs, LANES)), axis=1)

    def swap(x):
        return pltpu.roll(x, LANES // 2, 1)

    def cut(b):
        return slice(b * LANES, (b + 1) * LANES)

    for copy in scalar_copies:
        copy.wait()
    row0 = lax.broadcasted_iota(jnp.int32, (orbs, LANES), 0)
    column = jnp.zeros((orbs, LANES), F32)
    for o in range(orbs):
        column = jnp.where(row0 == o, relax * eigs[o], column)
    eg[...] = column
    lane1 = lax.broadcasted_iota(jnp.int32, (1, LANES), 1)
    perm_copy.wait()
    tcols[...] = jnp.zeros_like(tcols)
    tcols[:cells, :faces] = perm[...].astype(F32)
    tturn[...] = jnp.transpose(tcols[...])
    place = lax.broadcasted_iota(jnp.int32, (faces, LANES), 0).astype(F32)
    inverse = jnp.zeros((faces, LANES), F32)
    for k in range(faces):
        inverse = jnp.where(place == tturn[k : k + 1, :], float(k), inverse)
    tturn[:faces] = inverse
    tturn[faces:] = tturn[faces:] * 0.0
    inverse = jnp.transpose(tturn[...])[:cells]
    lanes = lax.broadcasted_iota(jnp.int32, (cells, LANES), 1)
    both = jnp.where(lanes < faces, inverse + faces, pltpu.roll(tcols[:cells], faces, 1))
    idx[...] = both.astype(jnp.int32)
    base_copy.wait()
    wb[...] = 1.0 - relax * base[...]

    def row_of(c):
        return idx[c : c + 1, :]

    def moved(value, product, c, b):
        return (wb[c : c + 1, cut(b)] + eg[...]) * value - (relax * scale[c]) * product

    src_copies[0].wait()
    src_copies[1].wait()
    at = list(range(ITERS)) + [cells - ITERS + s for s in range(ITERS)]
    for s, c in enumerate(at):
        edge[s] = src[c].astype(F32)
    stiff_copy.wait()
    for t in range(ITERS):
        count = ITERS - t
        live = list(range(count)) + list(range(2 * ITERS - count, 2 * ITERS))
        block = jnp.concatenate([edge[s] for s in live], axis=0).astype(BF16)
        if t == ITERS - 1:
            p0 = dot(block[:orbs], stiff[:, :LANES])
            p3 = dot(block[orbs:], stiff[:, last:])
            trace_l[t] = edge[0, :, :LANES] - moved(edge[0, :, :LANES], p0, 0, 0)
            s = 2 * ITERS - 1
            trace_r[t] = edge[s, :, last:] - moved(edge[s, :, last:], p3, end, parts - 1)
            break
        product = dot(block, stiff[...])
        q0, q3 = {}, {}
        for j, s in enumerate(live):
            c = at[s]
            for b in range(parts):
                value = edge[s, :, cut(b)]
                new = moved(value, product[j * orbs : (j + 1) * orbs, cut(b)], c, b)
                edge[s, :, cut(b)] = new + src[c, :, cut(b)].astype(F32)
                if b == 0:
                    q0[s] = value - new
                if b == parts - 1:
                    q3[s] = value - new
        trace_l[t] = q0[0]
        trace_r[t] = q3[2 * ITERS - 1]
        for j in range(len(live) - 1):
            s = live[j]
            if live[j + 1] == s + 1 and s != ITERS - 1:
                y = turned(jnp.where(low, q0[s + 1], q3[s]), row_of(at[s]))
                edge[s + 1, :, :LANES] = edge[s + 1, :, :LANES] - jnp.where(low, y, 0.0)
                edge[s, :, last:] = edge[s, :, last:] - jnp.where(low, 0.0, y)
    for k in range(ITERS // 2):
        a, b = trace_l[2 * k], trace_l[2 * k + 1]
        tx_l[k * orbs : (k + 1) * orbs] = jnp.where(low, a, swap(b))
        a, b = trace_r[2 * k], trace_r[2 * k + 1]
        tx_r[k * orbs : (k + 1) * orbs] = jnp.where(low, swap(a), b)
    meta = ITERS // 2 * orbs
    for buffer, near, far, pair in ((tx_l, 0, 1, 0), (tx_r, end, end - 1, end - 1)):
        buffer[meta:] = jnp.zeros_like(buffer[meta:])
        for b in range(parts):
            buffer[meta + b : meta + b + 1] = wb[near : near + 1, cut(b)]
            buffer[meta + parts + b : meta + parts + b + 1] = wb[far : far + 1, cut(b)]
        rest = meta + 2 * parts
        buffer[rest : rest + 1] = jnp.full((1, LANES), relax * scale[near], F32)
        buffer[rest + 1 : rest + 2] = jnp.full((1, LANES), relax * scale[far], F32)
        buffer[rest + 2 : rest + 3] = row_of(pair).astype(F32)
        buffer[rest + 3 : rest + 4] = row_of(end).astype(F32)
    pot_copy.wait()
    row = jnp.zeros((1, LANES), jnp.int32)
    for c in range(cells):
        row = jnp.where(lane1 == c, owner[c] * prow + slots[c], row)
    early[:phalf] = jnp.concatenate([pot[:phalf], pot[phalf:]], axis=1)
    early[phalf:] = jnp.broadcast_to(row.astype(F32), (8, LANES))
    pl.semaphore_wait(barrier, n - 1 + ranks - 1)

    @pl.when(has_left)
    def _():
        f_left.start()

    @pl.when(has_right)
    def _():
        f_right.start()

    def send_early(k, carry):
        early_copy(k).start()
        return carry

    def start_group(g, carry):
        span = pl.ds(g * group, group)
        it[span] = src[span].astype(F32)
        itb[span] = src[span]
        return carry

    src_copies[2].wait()
    lax.fori_loop(0, cells // group, start_group, 0)

    def stacked(buffer, span):
        if orbs % 16:
            return buffer[span].astype(F32).reshape(group * orbs, nodes).astype(BF16)
        return buffer[span].reshape(group * orbs, nodes)

    def sweep(final):
        before = None
        shift = eg[...]
        for g in range(cells // group):
            span = slice(g * group, (g + 1) * group)
            product = dot(stacked(itb, span), stiff[...])
            for k in range(group):
                c = g * group + k
                extra = c if c < ITERS else c - (cells - 2 * ITERS) if c >= cells - ITERS else None

                def put(c, b, value):
                    if final:
                        value = relax * value
                        adj[c, :, cut(b)] = value.astype(BF16)
                        dens[c : c + 1, cut(b)] = jnp.sum(psi[c, :, cut(b)].astype(F32) * value, axis=0, keepdims=True)
                    else:
                        it[c, :, cut(b)] = value
                        itb[c, :, cut(b)] = value.astype(BF16)

                for b in range(parts):
                    value, source = it[c, :, cut(b)], src[c, :, cut(b)].astype(F32)
                    kept = (wb[c : c + 1, cut(b)] + shift) * value
                    new = kept - (relax * scale[c]) * product[k * orbs : (k + 1) * orbs, cut(b)] + source
                    old = value + source - new
                    if final and extra is not None:
                        new = new + resp[extra, :, cut(b)]
                    if b == 0 and c > 0:
                        y = turned(jnp.where(low, old, before[0]), row_of(c - 1))
                        new = new - jnp.where(low, y, 0.0)
                        put(c - 1, parts - 1, before[1] - jnp.where(low, 0.0, y))
                    if b == parts - 1:
                        before = (old, new)
                    else:
                        put(c, b, new)
        put(end, parts - 1, before[1])

    shares = -(-(n - 1) // max(1, ITERS - 1))

    def free_sweep(t, carry):
        lax.fori_loop(jnp.minimum(n, 1 + t * shares), jnp.minimum(n, 1 + (t + 1) * shares), send_early, 0)
        sweep(False)
        return carry

    lax.fori_loop(0, ITERS - 1, free_sweep, 0)

    for copy in (psi_copy, restrict_copy, prolong_copy):
        copy.wait()

    @pl.when(has_left)
    def _():
        f_right.wait_recv()

    @pl.when(has_right)
    def _():
        f_left.wait_recv()

    def coming(has, buffer):
        return jnp.where(has, buffer[...], 0.0)

    in_r, in_l = coming(has_right, rx_r), coming(has_left, rx_l)
    rest = meta + 2 * parts

    def near_row(buffer, at):
        return buffer[at : at + 1]

    def ghosts(buffer):
        rows = [[near_row(buffer, meta + j * parts + b) for b in range(parts)] for j in range(2)]
        return [(rows[j], near_row(buffer, rest + j)) for j in range(2)]

    def owned(c):
        return [wb[c : c + 1, cut(b)] for b in range(parts)], relax * scale[c]

    ghost_r, ghost_l = ghosts(in_r), ghosts(in_l)
    pair_r = near_row(in_r, rest + 2).astype(jnp.int32)
    pair_l = near_row(in_l, rest + 2).astype(jnp.int32)
    joint_l = near_row(in_l, rest + 3).astype(jnp.int32)
    chain_r = [(ITERS + s, owned(cells - ITERS + s)) for s in range(ITERS)] + [(2 * ITERS + j, ghost_r[j]) for j in range(2)]
    chain_l = [(2 * ITERS + 3 - j, ghost_l[1 - j]) for j in range(2)] + [(s, owned(s)) for s in range(ITERS)]
    pairs_r = [row_of(cells - ITERS + s) for s in range(ITERS)] + [pair_r]
    pairs_l = [pair_l, joint_l] + [row_of(s) for s in range(ITERS - 1)]
    sides = ((chain_r, pairs_r, ITERS - 1, has_right), (chain_l, pairs_l, 1, has_left))

    def forcing(t):
        k, odd = t // 2, t % 2
        far = in_r[k * orbs : (k + 1) * orbs]
        far = swap(far) if odd else far
        y_r = turned(jnp.where(low, far, trace_r[t]), pairs_r[ITERS - 1])
        far = in_l[k * orbs : (k + 1) * orbs]
        far = far if odd else swap(far)
        y_l = turned(jnp.where(low, trace_l[t], far), joint_l)
        return jnp.where(has_right, y_r, 0.0), jnp.where(has_left, y_l, 0.0)

    for s in range(2 * ITERS + 4):
        resp[s] = jnp.zeros((orbs, nodes), F32)
    for t in range(ITERS):
        forced = forcing(t)
        live = []
        for chain, _, joint, _ in sides:
            first, stop = max(0, joint + 1 - t), min(len(chain), joint + 1 + t)
            if t == ITERS - 1:
                first, stop = 1, ITERS + 1
            live.append(list(range(first, stop)))
        if t > 0:
            stack = [resp[chain[j][0]] for (chain, _, _, _), js in zip(sides, live) for j in js]
            product = dot(jnp.concatenate(stack, axis=0).astype(BF16), stiff[...])
        offset = 0
        for (chain, pairs, joint, _), js, push in zip(sides, live, forced):
            q0, q3 = {}, {}
            for j in js:
                s, (rows, a) = chain[j]
                for b in range(parts):
                    value = resp[s, :, cut(b)]
                    new = (rows[b] + eg[...]) * value - a * product[offset : offset + orbs, cut(b)]
                    resp[s, :, cut(b)] = new
                    if b == 0:
                        q0[j] = value - new
                    if b == parts - 1:
                        q3[j] = value - new
                offset += orbs
            zero = jnp.zeros((orbs, LANES), F32)
            for j in range(len(chain) - 1):
                if j != joint and j not in q3 and j + 1 not in q0:
                    continue
                y = zero
                if j in q3 or j + 1 in q0:
                    y = turned(jnp.where(low, q0.get(j + 1, zero), q3.get(j, zero)), pairs[j])
                if j == joint:
                    y = y + push
                a, b = chain[j][0], chain[j + 1][0]
                resp[b, :, :LANES] = resp[b, :, :LANES] - jnp.where(low, y, 0.0)
                resp[a, :, last:] = resp[a, :, last:] - jnp.where(low, 0.0, y)

    sweep(True)
    d_hi, d_lo = split(dens[...])
    projected = dot_last(d_hi, restrict[...]) + dot_last(d_lo, restrict[...])
    rows = jnp.concatenate([projected[:half], projected[half:]], axis=1)
    own[...] = rows
    rows_all[d] = rows

    def send_rows(k, carry):
        at = k - 1 + jnp.where(k > d, 1, 0)
        rows_copy(lax.rem(at - d + n, n)).start()
        return carry

    lax.fori_loop(1, n, send_rows, 0)

    def apply_group(g, carry):
        block = psi[pl.ds(g * group, group)].astype(F32).reshape(group * orbs, nodes).astype(BF16)
        product = dot(block, stiff[...])
        for k in range(group):
            c = g * group + k
            part = product[k * orbs : (k + 1) * orbs]
            kin[c] = scale[c] * part + base[pl.ds(c, 1), :] * psi[c].astype(F32)
        return carry

    groups = cells // group
    apply_group(0, 0)
    apply_group(groups - 1, 0)
    ex_tl[...] = jnp.where(low, kin[0, :, :LANES], swap(psi[0].astype(F32)[:, :LANES]))
    ex_tr[...] = jnp.where(low, swap(kin[end, :, last:]), psi[end].astype(F32)[:, last:])

    @pl.when(has_left)
    def _():
        x_left.start()

    @pl.when(has_right)
    def _():
        x_right.start()

    lax.fori_loop(1, groups - 1, apply_group, 0)
    early_all[d] = early[...]

    def wait_early(k, carry):
        early_copy(k).wait()
        return carry

    lax.fori_loop(1, n, wait_early, 0)

    tcols[...] = jnp.zeros_like(tcols)

    def take_row(e, carry):
        tcols[pl.ds(e, 1), :] = early_all[e, phalf : phalf + 1, :]
        return carry

    lax.fori_loop(0, n, take_row, 0)
    tturn[...] = jnp.transpose(tcols[...])
    def spot(e, at):
        row = early_all[e, phalf : phalf + 1, :]
        return jnp.sum(jnp.where(lane1 == at, row, 0.0), axis=1, keepdims=True)

    wanted = early_all[d, phalf : phalf + 1, :]
    wanted = jnp.where(lane1 == cells, spot(jnp.maximum(d - 1, 0), cells - 1), wanted)
    wanted = jnp.where(lane1 == cells + 1, spot(jnp.minimum(d + 1, n - 1), 0), wanted)
    wanted = jnp.where(lane1 >= prow, (d * prow + lane1 - prow).astype(F32), wanted)
    for e in range(n):
        rows_e = pl.ds(e * half, half)
        mt_lo[rows_e, :] = (tturn[:half, e : e + 1] == wanted).astype(F32)
        mt_hi[rows_e, :] = (tturn[half : 2 * half, e : e + 1] == wanted).astype(F32)
    wanted_i = wanted.astype(jnp.int32)
    slot = wanted_i % prow
    spread = (wanted_i // prow) * phalf + slot % phalf
    hit = lax.broadcasted_iota(jnp.int32, (n * phalf, LANES), 0) == spread
    table = early_all[:, :phalf, :].reshape(n * phalf, LANES)
    t_hi, t_lo = split(table)
    hit_lo = jnp.where(hit & (slot < phalf), 1.0, 0.0).astype(BF16)
    hit_hi = jnp.where(hit & (slot >= phalf), 1.0, 0.0).astype(BF16)
    pot_rows = dot_first(hit_lo, t_hi) + dot_first(hit_lo, t_lo)
    pot_rows = pot_rows + pltpu.roll(dot_first(hit_hi, t_hi) + dot_first(hit_hi, t_lo), LANES // 2, 1)

    def wait_rows(k, carry):
        rows_copy(k).wait()
        return carry

    lax.fori_loop(1, n, wait_rows, 0)
    g_hi, g_lo = split(rows_all[...].reshape(n * half, LANES))
    m_lo, m_hi = mt_lo[...].astype(BF16), mt_hi[...].astype(BF16)
    total = dot_first(m_lo, g_hi) + dot_first(m_lo, g_lo)
    total = total + pltpu.roll(dot_first(m_hi, g_hi) + dot_first(m_hi, g_lo), LANES // 2, 1)
    lane64 = lax.broadcasted_iota(jnp.int32, (prow, LANES), 1)
    mine = jnp.where(lane64 < coarse, total[:prow], pltpu.roll(total[prow:], LANES // 2, 1))
    packed[...] = mine
    for k in range(1, ranks):
        rank_copy(k).start()
    for k in range(1, ranks):
        rank_copy(k).wait()
        mine = mine + packed_in[k]
    upd[...] = pot[...] - step_rate * pltpu.roll(mine, LANES // 2, 1)[:, :coarse]
    c_hi, c_lo = split((pot_rows[:prow] - step_rate * mine)[:, :coarse])
    node[...] = dot(c_hi, prolong[...]) + dot(c_lo, prolong[...])

    yl[...] = jnp.zeros_like(yl)
    yr[...] = jnp.zeros_like(yr)

    @pl.when(has_left)
    def _():
        x_right.wait_recv()
        far = swap(ex_l[...]) + node[cells : cells + 1, last:] * ex_l[...]
        y = turned(far, rx_l[rest + 3 : rest + 4].astype(jnp.int32))
        yl[...] = jnp.where(low, y, 0.0)

    @pl.when(has_right)
    def _():
        x_left.wait_recv()
        far = ex_r[...] + node[cells + 1 : cells + 2, :LANES] * swap(ex_r[...])
        y = turned(far, row_of(end))
        yr[...] = jnp.where(low, 0.0, y)

    @pl.when(has_left)
    def _():
        x_left.wait_send()
        f_left.wait_send()

    @pl.when(has_right)
    def _():
        x_right.wait_send()
        f_right.wait_send()


def finish(
    adj,
    upd,
    kin,
    psi,
    node,
    idx,
    yl,
    yr,
    adj_out,
    upd_out,
    app_out,
    app,
    sems,
):
    cells, orbs, nodes = psi.shape
    end = cells - 1
    parts = nodes // LANES
    group = 8 if cells % 8 == 0 else 1
    groups = cells // group
    adj_copy = pltpu.make_async_copy(adj, adj_out, sems.at[groups])
    upd_copy = pltpu.make_async_copy(upd, upd_out, sems.at[groups + 1])
    adj_copy.start()
    upd_copy.start()
    low = lax.broadcasted_iota(jnp.int32, (orbs, LANES), 1) < LANES // 2
    copies = []
    before = None
    start = 0
    for g in range(groups):
        for k in range(group):
            c = g * group + k
            for b in range(parts):
                at = slice(b * LANES, (b + 1) * LANES)
                value = kin[c, :, at] + node[c : c + 1, at] * psi[c, :, at].astype(F32)
                if b == 0:
                    if c == 0:
                        new = value + yl[...]
                    else:
                        row = jnp.broadcast_to(idx[c - 1 : c, :], (orbs, LANES))
                        y = jnp.take_along_axis(jnp.where(low, value, before), row, axis=1)
                        new = value + jnp.where(low, y, 0.0)
                        app[c - 1, :, nodes - LANES :] = (before + jnp.where(low, 0.0, y)).astype(BF16)
                    app[c, :, at] = new.astype(BF16)
                elif b == parts - 1:
                    before = value
                else:
                    app[c, :, at] = value.astype(BF16)
        stop = (g + 1) * group - 1
        if g == groups - 1:
            app[end, :, nodes - LANES :] = (before + yr[...]).astype(BF16)
            stop = cells
        if stop > start:
            span = pl.ds(start, stop - start)
            copies.append(pltpu.make_async_copy(app.at[span], app_out.at[span], sems.at[g]))
            copies[-1].start()
            start = stop
    adj_copy.wait()
    upd_copy.wait()
    for copy in copies:
        copy.wait()


def local(
    n,
    ranks,
    orbitals,
    adjoint_source,
    eigenvalues,
    cell_scale,
    base_potential,
    stiffness,
    face_perm,
    restrict,
    prolong,
    owner,
    pot_slot,
    potential,
):
    cells, orbs, nodes = orbitals.shape
    prow = potential.shape[0]
    vmem = pl.BlockSpec(memory_space=pltpu.VMEM)
    hbm = pl.BlockSpec(memory_space=pl.ANY)
    dma = pltpu.SemaphoreType.DMA
    half = cells // 2
    face = (orbs, LANES)
    shape = orbitals.shape
    meta = -(-(2 * (nodes // LANES) + 4) // 8) * 8
    message = (ITERS // 2 * orbs + meta, LANES)
    held = 8 * orbitals.size + 4 * (prow * nodes + cells * LANES + prow * LANES + 2 * orbs * LANES)
    room = min(60 * 2**20, 64 * 2**20 - held - 2**18) // 2**15 * 2**15
    results = pl.pallas_call(
        functools.partial(kernel, n, ranks),
        out_shape=(
            pltpu.VMEM(shape, BF16),
            pltpu.VMEM(potential.shape, F32),
            pltpu.VMEM(shape, F32),
            pltpu.VMEM(shape, BF16),
            pltpu.VMEM((prow, nodes), F32),
            pltpu.VMEM((cells, LANES), jnp.int32),
            pltpu.VMEM(face, F32),
            pltpu.VMEM(face, F32),
        ),
        in_specs=[hbm] * 12,
        out_specs=(vmem,) * 8,
        scratch_shapes=[
            pltpu.SMEM((orbs,), F32),
            pltpu.SMEM((cells,), F32),
            pltpu.SMEM((cells,), jnp.int32),
            pltpu.SMEM((cells,), jnp.int32),
            pltpu.VMEM(shape, BF16),
            pltpu.VMEM((cells, nodes), F32),
            pltpu.VMEM(stiffness.shape, BF16),
            pltpu.VMEM(face_perm.shape, jnp.int32),
            pltpu.VMEM(restrict.shape[::-1], BF16),
            pltpu.VMEM(prolong.shape, BF16),
            pltpu.VMEM(potential.shape, F32),
            pltpu.VMEM((prow // 2 + 8, LANES), F32),
            pltpu.VMEM(shape, F32),
            pltpu.VMEM(shape, BF16),
            pltpu.VMEM((cells, nodes), F32),
            pltpu.VMEM(face, F32),
            pltpu.VMEM((2 * ITERS, orbs, nodes), F32),
            pltpu.VMEM((2 * ITERS + 4, orbs, nodes), F32),
            pltpu.VMEM((ITERS,) + face, F32),
            pltpu.VMEM((ITERS,) + face, F32),
            pltpu.VMEM((cells, nodes), F32),
            pltpu.VMEM(message, F32),
            pltpu.VMEM(message, F32),
            pltpu.VMEM(message, F32),
            pltpu.VMEM(message, F32),
            pltpu.VMEM(face, F32),
            pltpu.VMEM(face, F32),
            pltpu.VMEM(face, F32),
            pltpu.VMEM(face, F32),
            pltpu.VMEM((n, prow // 2 + 8, LANES), F32),
            pltpu.VMEM((n, half, LANES), F32),
            pltpu.VMEM((half, LANES), F32),
            pltpu.VMEM((n * half, LANES), F32),
            pltpu.VMEM((n * half, LANES), F32),
            pltpu.VMEM((LANES, LANES), F32),
            pltpu.VMEM((LANES, LANES), F32),
            pltpu.VMEM((prow, LANES), F32),
            pltpu.VMEM((ranks, prow, LANES), F32),
            dma((2,)),
            dma((2,)),
            dma((2,)),
            dma((2,)),
            dma((n,)),
            dma((n,)),
            dma((n,)),
            dma((n,)),
            dma((ranks,)),
            dma((ranks,)),
            dma((14,)),
        ],
        compiler_params=pltpu.CompilerParams(collective_id=0, has_side_effects=True, vmem_limit_bytes=room),
    )(
        orbitals,
        adjoint_source,
        eigenvalues,
        cell_scale,
        base_potential,
        stiffness,
        face_perm,
        owner[:, 0],
        pot_slot,
        restrict.T,
        prolong,
        potential,
    )
    groups = cells // (8 if cells % 8 == 0 else 1)
    return pl.pallas_call(
        finish,
        out_shape=(
            jax.ShapeDtypeStruct(shape, BF16),
            jax.ShapeDtypeStruct(potential.shape, F32),
            jax.ShapeDtypeStruct(shape, BF16),
        ),
        in_specs=[vmem] * 8,
        out_specs=(hbm, hbm, hbm),
        scratch_shapes=[pltpu.VMEM(shape, BF16), dma((groups + 2,))],
        compiler_params=pltpu.CompilerParams(vmem_limit_bytes=8 * 2**20),
    )(*results)


def solution(mesh):
    in_specs = (
        P("dom", "orb", None),
        P("dom", "orb", None),
        P("orb"),
        P("dom"),
        P("dom", None),
        P(),
        P("dom", None),
        P(),
        P(),
        P("dom", None),
        P("dom"),
        P("dom", None),
    )
    out_specs = (P("dom", "orb", None), P("dom", None), P("dom", "orb", None))
    step = functools.partial(local, mesh.shape["dom"], mesh.shape["orb"])
    return jax.shard_map(step, mesh=mesh, in_specs=in_specs, out_specs=out_specs, check_vma=False)
```

```python
import functools

import jax
import jax.numpy as jnp
from jax import lax
from jax.experimental import pallas as pl
from jax.experimental.pallas import tpu as pltpu
from jax.sharding import PartitionSpec as P

ITERS = 4


relax = 0.25
step_rate = 0.1

LANES = 128
F32 = jnp.float32
BF16 = jnp.bfloat16


def split(x):
    hi = x.astype(BF16)
    return hi, (x - hi.astype(F32)).astype(BF16)


def dot(a, b):
    return jnp.dot(a, b, preferred_element_type=F32)


def dot_first(a, b):
    return lax.dot_general(a, b, (((0,), (0,)), ((), ())), preferred_element_type=F32)


def dot_last(a, b):
    return lax.dot_general(a, b, (((1,), (1,)), ((), ())), preferred_element_type=F32)


def kernel(
    n,
    ranks,
    psi_any,
    src_any,
    eigs_any,
    scale_any,
    base_any,
    stiff_any,
    perm_any,
    owner_any,
    slots_any,
    restrict_any,
    prolong_any,
    pot_any,
    adj,
    upd,
    kin,
    psi,
    node,
    idx,
    yl,
    yr,
    eigs,
    scale,
    owner,
    slots,
    src,
    base,
    stiff,
    perm,
    restrict,
    prolong,
    pot,
    early,
    it,
    itb,
    wb,
    eg,
    edge,
    resp,
    trace_l,
    trace_r,
    dens,
    tx_l,
    tx_r,
    rx_l,
    rx_r,
    ex_tl,
    ex_tr,
    ex_l,
    ex_r,
    early_all,
    rows_all,
    own,
    mt_lo,
    mt_hi,
    chosen,
    tcols,
    tturn,
    packed,
    packed_in,
    fs,
    fr,
    xs,
    xr,
    es,
    er,
    ps,
    pr,
    ws,
    wr,
    ins,
):
    cells, orbs, nodes = psi.shape
    end = cells - 1
    faces = perm.shape[1]
    half = cells // 2
    prow = pot.shape[0]
    phalf = prow // 2
    coarse = pot.shape[1]
    last = nodes - LANES
    parts = nodes // LANES
    group = 8 if cells % 8 == 0 else 1
    d = lax.axis_index("dom")
    r = lax.axis_index("orb")
    barrier = pltpu.get_barrier_semaphore()
    spans = ((0, ITERS), (cells - ITERS, ITERS), (ITERS, cells - 2 * ITERS))
    src_copies = [
        pltpu.make_async_copy(src_any.at[pl.ds(a, m)], src.at[pl.ds(a, m)], ins.at[k])
        for k, (a, m) in enumerate(spans)
    ]
    psi_copy = pltpu.make_async_copy(psi_any, psi, ins.at[3])
    small = ((stiff_any, stiff), (base_any, base), (perm_any, perm), (pot_any, pot), (restrict_any, restrict), (prolong_any, prolong))
    stiff_copy, base_copy, perm_copy, pot_copy, restrict_copy, prolong_copy = [
        pltpu.make_async_copy(a, b, ins.at[4 + k]) for k, (a, b) in enumerate(small)
    ]
    scalar = ((eigs_any, eigs), (scale_any, scale), (owner_any, owner), (slots_any, slots))
    scalar_copies = [pltpu.make_async_copy(a, b, ins.at[10 + k]) for k, (a, b) in enumerate(scalar)]
    for copy in scalar_copies:
        copy.start()
    for copy in (perm_copy, base_copy, src_copies[0], src_copies[1], stiff_copy, pot_copy, src_copies[2], psi_copy):
        copy.start()
    restrict_copy.start()
    prolong_copy.start()

    def greet_dom(k, carry):
        pl.semaphore_signal(barrier, inc=1, device_id={"dom": lax.rem(d + k, n)}, device_id_type=pl.DeviceIdType.MESH)
        return carry

    def greet_orb(k, carry):
        pl.semaphore_signal(barrier, inc=1, device_id={"orb": lax.rem(r + k, ranks)}, device_id_type=pl.DeviceIdType.MESH)
        return carry

    lax.fori_loop(1, n, greet_dom, 0)
    lax.fori_loop(1, ranks, greet_orb, 0)

    def send(source, target, s, t, where):
        return pltpu.make_async_remote_copy(
            src_ref=source,
            dst_ref=target,
            send_sem=s,
            recv_sem=t,
            device_id=where,
            device_id_type=pl.DeviceIdType.MESH,
        )

    right = {"dom": jnp.minimum(d + 1, n - 1)}
    left = {"dom": jnp.maximum(d - 1, 0)}
    has_right = d < n - 1
    has_left = d > 0
    f_left = send(tx_l, rx_r, fs.at[0], fr.at[0], left)
    f_right = send(tx_r, rx_l, fs.at[1], fr.at[1], right)
    x_left = send(ex_tl, ex_r, xs.at[0], xr.at[0], left)
    x_right = send(ex_tr, ex_l, xs.at[1], xr.at[1], right)

    def early_copy(k):
        return send(early, early_all.at[d], es.at[k], er.at[k], {"dom": lax.rem(d + k, n)})

    def rows_copy(k):
        return send(own, rows_all.at[d], ps.at[k], pr.at[k], {"dom": lax.rem(d + k, n)})

    def rank_copy(k):
        return send(packed, packed_in.at[k], ws.at[k], wr.at[k], {"orb": lax.rem(r + k, ranks)})

    lane = lax.broadcasted_iota(jnp.int32, (orbs, LANES), 1)
    low = lane < LANES // 2

    def turned(x, row):
        return jnp.take_along_axis(x, jnp.broadcast_to(row, (orbs, LANES)), axis=1)

    def swap(x):
        return pltpu.roll(x, LANES // 2, 1)

    def cut(b):
        return slice(b * LANES, (b + 1) * LANES)

    for copy in scalar_copies:
        copy.wait()
    row0 = lax.broadcasted_iota(jnp.int32, (orbs, LANES), 0)
    column = jnp.zeros((orbs, LANES), F32)
    for o in range(orbs):
        column = jnp.where(row0 == o, relax * eigs[o], column)
    eg[...] = column
    lane1 = lax.broadcasted_iota(jnp.int32, (1, LANES), 1)
    perm_copy.wait()
    tcols[...] = jnp.zeros_like(tcols)
    tcols[:cells, :faces] = perm[...].astype(F32)
    tturn[...] = jnp.transpose(tcols[...])
    place = lax.broadcasted_iota(jnp.int32, (faces, LANES), 0).astype(F32)
    inverse = jnp.zeros((faces, LANES), F32)
    for k in range(faces):
        inverse = jnp.where(place == tturn[k : k + 1, :], float(k), inverse)
    tturn[:faces] = inverse
    tturn[faces:] = tturn[faces:] * 0.0
    inverse = jnp.transpose(tturn[...])[:cells]
    lanes = lax.broadcasted_iota(jnp.int32, (cells, LANES), 1)
    both = jnp.where(lanes < faces, inverse + faces, pltpu.roll(tcols[:cells], faces, 1))
    idx[...] = both.astype(jnp.int32)
    base_copy.wait()
    wb[...] = 1.0 - relax * base[...]

    def row_of(c):
        return idx[c : c + 1, :]

    def moved(value, product, c, b):
        return (wb[c : c + 1, cut(b)] + eg[...]) * value - (relax * scale[c]) * product

    src_copies[0].wait()
    src_copies[1].wait()
    at = list(range(ITERS)) + [cells - ITERS + s for s in range(ITERS)]
    for s, c in enumerate(at):
        edge[s] = src[c].astype(F32)
    stiff_copy.wait()
    for t in range(ITERS):
        count = ITERS - t
        live = list(range(count)) + list(range(2 * ITERS - count, 2 * ITERS))
        block = jnp.concatenate([edge[s] for s in live], axis=0).astype(BF16)
        if t == ITERS - 1:
            p0 = dot(block[:orbs], stiff[:, :LANES])
            p3 = dot(block[orbs:], stiff[:, last:])
            trace_l[t] = edge[0, :, :LANES] - moved(edge[0, :, :LANES], p0, 0, 0)
            s = 2 * ITERS - 1
            trace_r[t] = edge[s, :, last:] - moved(edge[s, :, last:], p3, end, parts - 1)
            break
        product = dot(block, stiff[...])
        q0, q3 = {}, {}
        for j, s in enumerate(live):
            c = at[s]
            for b in range(parts):
                value = edge[s, :, cut(b)]
                new = moved(value, product[j * orbs : (j + 1) * orbs, cut(b)], c, b)
                edge[s, :, cut(b)] = new + src[c, :, cut(b)].astype(F32)
                if b == 0:
                    q0[s] = value - new
                if b == parts - 1:
                    q3[s] = value - new
        trace_l[t] = q0[0]
        trace_r[t] = q3[2 * ITERS - 1]
        for j in range(len(live) - 1):
            s = live[j]
            if live[j + 1] == s + 1 and s != ITERS - 1:
                y = turned(jnp.where(low, q0[s + 1], q3[s]), row_of(at[s]))
                edge[s + 1, :, :LANES] = edge[s + 1, :, :LANES] - jnp.where(low, y, 0.0)
                edge[s, :, last:] = edge[s, :, last:] - jnp.where(low, 0.0, y)
    for k in range(ITERS // 2):
        a, b = trace_l[2 * k], trace_l[2 * k + 1]
        tx_l[k * orbs : (k + 1) * orbs] = jnp.where(low, a, swap(b))
        a, b = trace_r[2 * k], trace_r[2 * k + 1]
        tx_r[k * orbs : (k + 1) * orbs] = jnp.where(low, swap(a), b)
    meta = ITERS // 2 * orbs
    for buffer, near, far, pair in ((tx_l, 0, 1, 0), (tx_r, end, end - 1, end - 1)):
        buffer[meta:] = jnp.zeros_like(buffer[meta:])
        for b in range(parts):
            buffer[meta + b : meta + b + 1] = wb[near : near + 1, cut(b)]
            buffer[meta + parts + b : meta + parts + b + 1] = wb[far : far + 1, cut(b)]
        rest = meta + 2 * parts
        buffer[rest : rest + 1] = jnp.full((1, LANES), relax * scale[near], F32)
        buffer[rest + 1 : rest + 2] = jnp.full((1, LANES), relax * scale[far], F32)
        buffer[rest + 2 : rest + 3] = row_of(pair).astype(F32)
        buffer[rest + 3 : rest + 4] = row_of(end).astype(F32)
    pot_copy.wait()
    row = jnp.zeros((1, LANES), jnp.int32)
    for c in range(cells):
        row = jnp.where(lane1 == c, owner[c] * prow + slots[c], row)
    early[:phalf] = jnp.concatenate([pot[:phalf], pot[phalf:]], axis=1)
    early[phalf:] = jnp.broadcast_to(row.astype(F32), (8, LANES))
    pl.semaphore_wait(barrier, n - 1 + ranks - 1)

    @pl.when(has_left)
    def _():
        f_left.start()

    @pl.when(has_right)
    def _():
        f_right.start()

    def send_early(k, carry):
        early_copy(k).start()
        return carry

    def start_group(g, carry):
        span = pl.ds(g * group, group)
        it[span] = src[span].astype(F32)
        itb[span] = src[span]
        return carry

    src_copies[2].wait()
    lax.fori_loop(0, cells // group, start_group, 0)

    def stacked(buffer, span):
        if orbs % 16:
            return buffer[span].astype(F32).reshape(group * orbs, nodes).astype(BF16)
        return buffer[span].reshape(group * orbs, nodes)

    def sweep(final):
        before = None
        shift = eg[...]
        for g in range(cells // group):
            span = slice(g * group, (g + 1) * group)
            product = dot(stacked(itb, span), stiff[...])
            for k in range(group):
                c = g * group + k
                extra = c if c < ITERS else c - (cells - 2 * ITERS) if c >= cells - ITERS else None

                def put(c, b, value):
                    if final:
                        value = relax * value
                        adj[c, :, cut(b)] = value.astype(BF16)
                        dens[c : c + 1, cut(b)] = jnp.sum(psi[c, :, cut(b)].astype(F32) * value, axis=0, keepdims=True)
                    else:
                        it[c, :, cut(b)] = value
                        itb[c, :, cut(b)] = value.astype(BF16)

                for b in range(parts):
                    value, source = it[c, :, cut(b)], src[c, :, cut(b)].astype(F32)
                    kept = (wb[c : c + 1, cut(b)] + shift) * value
                    new = kept - (relax * scale[c]) * product[k * orbs : (k + 1) * orbs, cut(b)] + source
                    old = value + source - new
                    if final and extra is not None:
                        new = new + resp[extra, :, cut(b)]
                    if b == 0 and c > 0:
                        y = turned(jnp.where(low, old, before[0]), row_of(c - 1))
                        new = new - jnp.where(low, y, 0.0)
                        put(c - 1, parts - 1, before[1] - jnp.where(low, 0.0, y))
                    if b == parts - 1:
                        before = (old, new)
                    else:
                        put(c, b, new)
        put(end, parts - 1, before[1])

    shares = -(-(n - 1) // max(1, ITERS - 1))

    def free_sweep(t, carry):
        lax.fori_loop(jnp.minimum(n, 1 + t * shares), jnp.minimum(n, 1 + (t + 1) * shares), send_early, 0)
        sweep(False)
        return carry

    lax.fori_loop(0, ITERS - 1, free_sweep, 0)

    for copy in (psi_copy, restrict_copy, prolong_copy):
        copy.wait()

    @pl.when(has_left)
    def _():
        f_right.wait_recv()

    @pl.when(has_right)
    def _():
        f_left.wait_recv()

    def coming(has, buffer):
        return jnp.where(has, buffer[...], 0.0)

    in_r, in_l = coming(has_right, rx_r), coming(has_left, rx_l)
    rest = meta + 2 * parts

    def near_row(buffer, at):
        return buffer[at : at + 1]

    def ghosts(buffer):
        rows = [[near_row(buffer, meta + j * parts + b) for b in range(parts)] for j in range(2)]
        return [(rows[j], near_row(buffer, rest + j)) for j in range(2)]

    def owned(c):
        return [wb[c : c + 1, cut(b)] for b in range(parts)], relax * scale[c]

    ghost_r, ghost_l = ghosts(in_r), ghosts(in_l)
    pair_r = near_row(in_r, rest + 2).astype(jnp.int32)
    pair_l = near_row(in_l, rest + 2).astype(jnp.int32)
    joint_l = near_row(in_l, rest + 3).astype(jnp.int32)
    chain_r = [(ITERS + s, owned(cells - ITERS + s)) for s in range(ITERS)] + [(2 * ITERS + j, ghost_r[j]) for j in range(2)]
    chain_l = [(2 * ITERS + 3 - j, ghost_l[1 - j]) for j in range(2)] + [(s, owned(s)) for s in range(ITERS)]
    pairs_r = [row_of(cells - ITERS + s) for s in range(ITERS)] + [pair_r]
    pairs_l = [pair_l, joint_l] + [row_of(s) for s in range(ITERS - 1)]
    sides = ((chain_r, pairs_r, ITERS - 1, has_right), (chain_l, pairs_l, 1, has_left))

    def forcing(t):
        k, odd = t // 2, t % 2
        far = in_r[k * orbs : (k + 1) * orbs]
        far = swap(far) if odd else far
        y_r = turned(jnp.where(low, far, trace_r[t]), pairs_r[ITERS - 1])
        far = in_l[k * orbs : (k + 1) * orbs]
        far = far if odd else swap(far)
        y_l = turned(jnp.where(low, trace_l[t], far), joint_l)
        return jnp.where(has_right, y_r, 0.0), jnp.where(has_left, y_l, 0.0)

    for s in range(2 * ITERS + 4):
        resp[s] = jnp.zeros((orbs, nodes), F32)
    for t in range(ITERS):
        forced = forcing(t)
        live = []
        for chain, _, joint, _ in sides:
            first, stop = max(0, joint + 1 - t), min(len(chain), joint + 1 + t)
            if t == ITERS - 1:
                first, stop = 1, ITERS + 1
            live.append(list(range(first, stop)))
        if t > 0:
            stack = [resp[chain[j][0]] for (chain, _, _, _), js in zip(sides, live) for j in js]
            product = dot(jnp.concatenate(stack, axis=0).astype(BF16), stiff[...])
        offset = 0
        for (chain, pairs, joint, _), js, push in zip(sides, live, forced):
            q0, q3 = {}, {}
            for j in js:
                s, (rows, a) = chain[j]
                for b in range(parts):
                    value = resp[s, :, cut(b)]
                    new = (rows[b] + eg[...]) * value - a * product[offset : offset + orbs, cut(b)]
                    resp[s, :, cut(b)] = new
                    if b == 0:
                        q0[j] = value - new
                    if b == parts - 1:
                        q3[j] = value - new
                offset += orbs
            zero = jnp.zeros((orbs, LANES), F32)
            for j in range(len(chain) - 1):
                if j != joint and j not in q3 and j + 1 not in q0:
                    continue
                y = zero
                if j in q3 or j + 1 in q0:
                    y = turned(jnp.where(low, q0.get(j + 1, zero), q3.get(j, zero)), pairs[j])
                if j == joint:
                    y = y + push
                a, b = chain[j][0], chain[j + 1][0]
                resp[b, :, :LANES] = resp[b, :, :LANES] - jnp.where(low, y, 0.0)
                resp[a, :, last:] = resp[a, :, last:] - jnp.where(low, 0.0, y)

    sweep(True)
    d_hi, d_lo = split(dens[...])
    projected = dot_last(d_hi, restrict[...]) + dot_last(d_lo, restrict[...])
    rows = jnp.concatenate([projected[:half], projected[half:]], axis=1)
    own[...] = rows
    rows_all[d] = rows

    def send_rows(k, carry):
        at = k - 1 + jnp.where(k > d, 1, 0)
        rows_copy(lax.rem(at - d + n, n)).start()
        return carry

    lax.fori_loop(1, n, send_rows, 0)

    def apply_group(g, carry):
        product = dot(stacked(psi, pl.ds(g * group, group)), stiff[...])
        for k in range(group):
            c = g * group + k
            part = product[k * orbs : (k + 1) * orbs]
            kin[c] = scale[c] * part + base[pl.ds(c, 1), :] * psi[c].astype(F32)
        return carry

    groups = cells // group
    apply_group(0, 0)
    apply_group(groups - 1, 0)
    ex_tl[...] = jnp.where(low, kin[0, :, :LANES], swap(psi[0].astype(F32)[:, :LANES]))
    ex_tr[...] = jnp.where(low, swap(kin[end, :, last:]), psi[end].astype(F32)[:, last:])

    @pl.when(has_left)
    def _():
        x_left.start()

    @pl.when(has_right)
    def _():
        x_right.start()

    lax.fori_loop(1, groups - 1, apply_group, 0)
    early_all[d] = early[...]

    def wait_early(k, carry):
        early_copy(k).wait()
        return carry

    lax.fori_loop(1, n, wait_early, 0)

    tcols[...] = jnp.zeros_like(tcols)

    def take_row(e, carry):
        tcols[pl.ds(e, 1), :] = early_all[e, phalf : phalf + 1, :]
        return carry

    lax.fori_loop(0, n, take_row, 0)
    tturn[...] = jnp.transpose(tcols[...])
    def spot(e, at):
        row = early_all[e, phalf : phalf + 1, :]
        return jnp.sum(jnp.where(lane1 == at, row, 0.0), axis=1, keepdims=True)

    wanted = early_all[d, phalf : phalf + 1, :]
    wanted = jnp.where(lane1 == cells, spot(jnp.maximum(d - 1, 0), cells - 1), wanted)
    wanted = jnp.where(lane1 == cells + 1, spot(jnp.minimum(d + 1, n - 1), 0), wanted)
    wanted = jnp.where(lane1 >= prow, (d * prow + lane1 - prow).astype(F32), wanted)
    for e in range(n):
        rows_e = pl.ds(e * half, half)
        mt_lo[rows_e, :] = (tturn[:half, e : e + 1] == wanted).astype(F32)
        mt_hi[rows_e, :] = (tturn[half : 2 * half, e : e + 1] == wanted).astype(F32)
    chosen[:LANES] = jnp.transpose(mt_lo[...]).astype(BF16)
    chosen[LANES:] = jnp.transpose(mt_hi[...]).astype(BF16)
    wanted_i = wanted.astype(jnp.int32)
    slot = wanted_i % prow
    spread = (wanted_i // prow) * phalf + slot % phalf
    hit = lax.broadcasted_iota(jnp.int32, (n * phalf, LANES), 0) == spread
    table = early_all[:, :phalf, :].reshape(n * phalf, LANES)
    t_hi, t_lo = split(table)
    hit_lo = jnp.where(hit & (slot < phalf), 1.0, 0.0).astype(BF16)
    hit_hi = jnp.where(hit & (slot >= phalf), 1.0, 0.0).astype(BF16)
    pot_rows = dot_first(hit_lo, t_hi) + dot_first(hit_lo, t_lo)
    pot_rows = pot_rows + pltpu.roll(dot_first(hit_hi, t_hi) + dot_first(hit_hi, t_lo), LANES // 2, 1)

    def wait_rows(k, carry):
        rows_copy(k).wait()
        return carry

    lax.fori_loop(1, n, wait_rows, 0)
    g_hi, g_lo = split(rows_all[...].reshape(n * half, LANES))
    sums = dot(chosen[...], jnp.concatenate([g_hi, g_lo], axis=1))
    sums = sums[:, :LANES] + sums[:, LANES:]
    total = sums[:LANES] + pltpu.roll(sums[LANES:], LANES // 2, 1)
    lane64 = lax.broadcasted_iota(jnp.int32, (prow, LANES), 1)
    mine = jnp.where(lane64 < coarse, total[:prow], pltpu.roll(total[prow:], LANES // 2, 1))
    packed[...] = mine
    for k in range(1, ranks):
        rank_copy(k).start()
    for k in range(1, ranks):
        rank_copy(k).wait()
        mine = mine + packed_in[k]
    upd[...] = pot[...] - step_rate * pltpu.roll(mine, LANES // 2, 1)[:, :coarse]
    c_hi, c_lo = split((pot_rows[:prow] - step_rate * mine)[:, :coarse])
    node[...] = dot(c_hi, prolong[...]) + dot(c_lo, prolong[...])

    yl[...] = jnp.zeros_like(yl)
    yr[...] = jnp.zeros_like(yr)

    @pl.when(has_left)
    def _():
        x_right.wait_recv()
        far = swap(ex_l[...]) + node[cells : cells + 1, last:] * ex_l[...]
        y = turned(far, rx_l[rest + 3 : rest + 4].astype(jnp.int32))
        yl[...] = jnp.where(low, y, 0.0)

    @pl.when(has_right)
    def _():
        x_left.wait_recv()
        far = ex_r[...] + node[cells + 1 : cells + 2, :LANES] * swap(ex_r[...])
        y = turned(far, row_of(end))
        yr[...] = jnp.where(low, 0.0, y)

    @pl.when(has_left)
    def _():
        x_left.wait_send()
        f_left.wait_send()

    @pl.when(has_right)
    def _():
        x_right.wait_send()
        f_right.wait_send()


def finish(
    adj,
    upd,
    kin,
    psi,
    node,
    idx,
    yl,
    yr,
    adj_out,
    upd_out,
    app_out,
    app,
    sems,
):
    cells, orbs, nodes = psi.shape
    end = cells - 1
    parts = nodes // LANES
    group = 8 if cells % 8 == 0 else 1
    groups = cells // group
    adj_copy = pltpu.make_async_copy(adj, adj_out, sems.at[groups])
    upd_copy = pltpu.make_async_copy(upd, upd_out, sems.at[groups + 1])
    adj_copy.start()
    upd_copy.start()
    low = lax.broadcasted_iota(jnp.int32, (orbs, LANES), 1) < LANES // 2
    copies = []
    before = None
    start = 0
    for g in range(groups):
        for k in range(group):
            c = g * group + k
            for b in range(parts):
                at = slice(b * LANES, (b + 1) * LANES)
                value = kin[c, :, at] + node[c : c + 1, at] * psi[c, :, at].astype(F32)
                if b == 0:
                    if c == 0:
                        new = value + yl[...]
                    else:
                        row = jnp.broadcast_to(idx[c - 1 : c, :], (orbs, LANES))
                        y = jnp.take_along_axis(jnp.where(low, value, before), row, axis=1)
                        new = value + jnp.where(low, y, 0.0)
                        app[c - 1, :, nodes - LANES :] = (before + jnp.where(low, 0.0, y)).astype(BF16)
                    app[c, :, at] = new.astype(BF16)
                elif b == parts - 1:
                    before = value
                else:
                    app[c, :, at] = value.astype(BF16)
        stop = (g + 1) * group - 1
        if g == groups - 1:
            app[end, :, nodes - LANES :] = (before + yr[...]).astype(BF16)
            stop = cells
        if stop > start:
            span = pl.ds(start, stop - start)
            copies.append(pltpu.make_async_copy(app.at[span], app_out.at[span], sems.at[g]))
            copies[-1].start()
            start = stop
    adj_copy.wait()
    upd_copy.wait()
    for copy in copies:
        copy.wait()


def local(
    n,
    ranks,
    orbitals,
    adjoint_source,
    eigenvalues,
    cell_scale,
    base_potential,
    stiffness,
    face_perm,
    restrict,
    prolong,
    owner,
    pot_slot,
    potential,
):
    cells, orbs, nodes = orbitals.shape
    prow = potential.shape[0]
    vmem = pl.BlockSpec(memory_space=pltpu.VMEM)
    hbm = pl.BlockSpec(memory_space=pl.ANY)
    dma = pltpu.SemaphoreType.DMA
    half = cells // 2
    face = (orbs, LANES)
    shape = orbitals.shape
    meta = -(-(2 * (nodes // LANES) + 4) // 8) * 8
    message = (ITERS // 2 * orbs + meta, LANES)
    held = 8 * orbitals.size + 4 * (prow * nodes + cells * LANES + prow * LANES + 2 * orbs * LANES)
    room = min(60 * 2**20, 64 * 2**20 - held - 2**18) // 2**15 * 2**15
    results = pl.pallas_call(
        functools.partial(kernel, n, ranks),
        out_shape=(
            pltpu.VMEM(shape, BF16),
            pltpu.VMEM(potential.shape, F32),
            pltpu.VMEM(shape, F32),
            pltpu.VMEM(shape, BF16),
            pltpu.VMEM((prow, nodes), F32),
            pltpu.VMEM((cells, LANES), jnp.int32),
            pltpu.VMEM(face, F32),
            pltpu.VMEM(face, F32),
        ),
        in_specs=[hbm] * 12,
        out_specs=(vmem,) * 8,
        scratch_shapes=[
            pltpu.SMEM((orbs,), F32),
            pltpu.SMEM((cells,), F32),
            pltpu.SMEM((cells,), jnp.int32),
            pltpu.SMEM((cells,), jnp.int32),
            pltpu.VMEM(shape, BF16),
            pltpu.VMEM((cells, nodes), F32),
            pltpu.VMEM(stiffness.shape, BF16),
            pltpu.VMEM(face_perm.shape, jnp.int32),
            pltpu.VMEM(restrict.shape[::-1], BF16),
            pltpu.VMEM(prolong.shape, BF16),
            pltpu.VMEM(potential.shape, F32),
            pltpu.VMEM((prow // 2 + 8, LANES), F32),
            pltpu.VMEM(shape, F32),
            pltpu.VMEM(shape, BF16),
            pltpu.VMEM((cells, nodes), F32),
            pltpu.VMEM(face, F32),
            pltpu.VMEM((2 * ITERS, orbs, nodes), F32),
            pltpu.VMEM((2 * ITERS + 4, orbs, nodes), F32),
            pltpu.VMEM((ITERS,) + face, F32),
            pltpu.VMEM((ITERS,) + face, F32),
            pltpu.VMEM((cells, nodes), F32),
            pltpu.VMEM(message, F32),
            pltpu.VMEM(message, F32),
            pltpu.VMEM(message, F32),
            pltpu.VMEM(message, F32),
            pltpu.VMEM(face, F32),
            pltpu.VMEM(face, F32),
            pltpu.VMEM(face, F32),
            pltpu.VMEM(face, F32),
            pltpu.VMEM((n, prow // 2 + 8, LANES), F32),
            pltpu.VMEM((n, half, LANES), F32),
            pltpu.VMEM((half, LANES), F32),
            pltpu.VMEM((n * half, LANES), F32),
            pltpu.VMEM((n * half, LANES), F32),
            pltpu.VMEM((2 * LANES, n * half), BF16),
            pltpu.VMEM((LANES, LANES), F32),
            pltpu.VMEM((LANES, LANES), F32),
            pltpu.VMEM((prow, LANES), F32),
            pltpu.VMEM((ranks, prow, LANES), F32),
            dma((2,)),
            dma((2,)),
            dma((2,)),
            dma((2,)),
            dma((n,)),
            dma((n,)),
            dma((n,)),
            dma((n,)),
            dma((ranks,)),
            dma((ranks,)),
            dma((14,)),
        ],
        compiler_params=pltpu.CompilerParams(collective_id=0, has_side_effects=True, vmem_limit_bytes=room),
    )(
        orbitals,
        adjoint_source,
        eigenvalues,
        cell_scale,
        base_potential,
        stiffness,
        face_perm,
        owner[:, 0],
        pot_slot,
        restrict.T,
        prolong,
        potential,
    )
    groups = cells // (8 if cells % 8 == 0 else 1)
    return pl.pallas_call(
        finish,
        out_shape=(
            jax.ShapeDtypeStruct(shape, BF16),
            jax.ShapeDtypeStruct(potential.shape, F32),
            jax.ShapeDtypeStruct(shape, BF16),
        ),
        in_specs=[vmem] * 8,
        out_specs=(hbm, hbm, hbm),
        scratch_shapes=[pltpu.VMEM(shape, BF16), dma((groups + 2,))],
        compiler_params=pltpu.CompilerParams(vmem_limit_bytes=8 * 2**20),
    )(*results)


def solution(mesh):
    in_specs = (
        P("dom", "orb", None),
        P("dom", "orb", None),
        P("orb"),
        P("dom"),
        P("dom", None),
        P(),
        P("dom", None),
        P(),
        P(),
        P("dom", None),
        P("dom"),
        P("dom", None),
    )
    out_specs = (P("dom", "orb", None), P("dom", None), P("dom", "orb", None))
    step = functools.partial(local, mesh.shape["dom"], mesh.shape["orb"])
    return jax.shard_map(step, mesh=mesh, in_specs=in_specs, out_specs=out_specs, check_vma=False)
```
